32 devices in a mesh: clip: 4 (over x, core), tm: 8 (over z, y).
Axes of the slice: x: 2, y: 2, z: 4, core: 2. Of those that a mesh axis runs over, the one named last changes fastest.
Arguments:
- inputs: bfloat16 [4, 2560, 768], P('clip', 'tm'), may hold values from -6 to 6
- query_states: bfloat16 [4, 2560, 768], P('clip', 'tm'), may hold values from -9 to 9
- key_states: bfloat16 [4, 2560, 768], P('clip', 'tm'), may hold values from -9 to 9
- value_states: bfloat16 [4, 2560, 768], P('clip', 'tm'), may hold values from -6 to 6
- out_grad: bfloat16 [4, 2560, 768], P('clip', 'tm'), may hold values from -1.1953125 to 1.1953125
- first_flags: int32 [4, 8], P('clip'), may hold values from 0 to 1, as said below
- weight: float32 [768, 768], P('tm'), may hold values from -1.2 to 1.2
- moment_one: float32 [768, 768], P('tm'), may hold values from -6 to 6
- moment_two: float32 [768, 768], P('tm'), may hold values from 0.25 to 4
Outputs:
- new_weight: float32 [768, 768], P('tm')
- new_moment_one: float32 [768, 768], P('tm')
- new_moment_two: float32 [768, 768], P('tm')
The draws below stay inside these ranges and needn't reach their ends.
Inputs may be any that keep to these rules, and one draw needn't show every extreme that they name: `first_flags`: the first frame of every sequence has flag 1.
All inputs are finite; a program needn't handle non-finite values.
Results may differ from the reference program's by a relative error of at most 0.0044.
Values may be sent and summed in bfloat16 or wider, within the bound.
No kernel may reach another device: no remote copies, remote signals or barrier semaphores. Data moves between devices by JAX's collectives and lax.ppermute only.
A program may use at most 64 MiB of HBM per device.

```python
import math
import jax
import jax.numpy as jnp
from jax import lax

HEAD_DIM = 128
HEADS = 6
DX = 768
FRAME_TOK = 320
ATT = 768
FRAMES = 8
SEQS = 4
TOKENS = 2560


def drawn_pair(key):
    shape = (SEQS, TOKENS, ATT)
    key_part = jnp.clip(jax.random.normal(jax.random.fold_in(key, 11), shape, jnp.float32), -6.0, 6.0)
    query_part = jnp.clip(jax.random.normal(jax.random.fold_in(key, 12), shape, jnp.float32), -6.0, 6.0)
    return (query_part, key_part)


def draw_query_states(key, part):
    return drawn_pair(key)[0].astype(jnp.bfloat16)


def draw_key_states(key, part):
    return drawn_pair(key)[1].astype(jnp.bfloat16)


def draw_first_flags(key, part):
    draws = jax.random.randint(jax.random.fold_in(key, 21), (SEQS, FRAMES), 0, 8)
    flag_rows = jnp.where(draws == 0, 1, 0).astype(jnp.int32)
    return flag_rows.at[:, 0].set(1)


def strengthened(values, rng, source, target, blocks, factor):
    owner, partner = [(jnp.arange(values.shape[dim]) // (values.shape[dim] // blocks)).reshape([-1 if axis == dim else 1 for axis in range(values.ndim)]) for dim in (source, target)]
    chosen = jax.random.permutation(rng, blocks)[partner]
    strong = (owner == chosen) | (owner == (partner + blocks // 2) % blocks)
    return jnp.where(strong, factor * values, values)


def block_scale(rng, extent, split, least, high):
    level, own = 1.0, jax.random.fold_in(rng, 6)
    for dim, shards_of in split:
        steps = jnp.exp(jax.random.uniform(jax.random.fold_in(own, dim), (shards_of,), jnp.float32, least / len(split), high / len(split)))
        level = level * jnp.repeat(steps, extent[dim] // shards_of).reshape([-1 if axis == dim else 1 for axis in range(len(extent))])
    return level


def centred(rng, shape, width, most, cuts=(), kind=jnp.bfloat16):
    drawn = jax.random.normal(rng, shape, jnp.float32) * width
    if len(cuts) > 0:
        drawn = block_scale(rng, shape, cuts, -0.22, 0.18) * drawn
    return jnp.clip(drawn, min=-most, max=most).astype(kind)


def bell_draw_with(rng, shape, width, most, shards, heavy, held_as=jnp.bfloat16):
    array = width * jax.random.normal(rng, shape, jnp.float32)
    if shards:
        array = array * block_scale(rng, shape, shards, -0.22, 0.18)
    return jnp.clip(strengthened(array, jax.random.fold_in(rng, 3), *heavy), -most, most).astype(held_as)


def setup_inputs(seed: int = 0) -> dict:
    key_of = jax.random.split(jax.random.key(seed), 10)
    return {
        "inputs": bell_draw_with(key_of[0], (SEQS, TOKENS, DX), 1.0, 6.0, ((0, 4), (1, 8)), (1, 2, 8, 2.0)),
        "query_states": draw_query_states(jax.random.fold_in(key_of[9], 71), 0),
        "key_states": draw_key_states(jax.random.fold_in(key_of[9], 71), 0),
        "value_states": centred(key_of[3], (SEQS, TOKENS, ATT), 1.0, 6.0, ((0, 4), (1, 8))),
        "out_grad": centred(key_of[4], (SEQS, TOKENS, ATT), 0.2, 1.1953125, ((0, 4), (1, 8))),
        "first_flags": draw_first_flags(jax.random.fold_in(key_of[9], 71), 0),
        "weight": centred(key_of[6], (DX, ATT), 0.2, 1.2, ((0, 8),), jnp.float32),
        "moment_one": centred(key_of[7], (DX, ATT), 1.0, 6.0, ((0, 8),), jnp.float32),
        "moment_two": jnp.clip(jnp.exp(math.log(4.0) - 2.7725887 * jax.random.uniform(key_of[8], (DX, ATT), jnp.float32) ** block_scale(key_of[8], (DX, ATT), ((0, 8),), -0.2, 0.2)), 0.25, 4.0),
    }


beta_one = 0.9
beta_two = 0.95
learn_rate = 0.001
adam_eps = 1e-08
decay_rate = 0.1
step_count = 10.0

def adamw(weight, moment_one, moment_two, gradient):
    new_one = beta_one * moment_one + (1.0 - beta_one) * gradient
    new_two = beta_two * moment_two + (1.0 - beta_two) * gradient * gradient
    corr_one = new_one / (1.0 - beta_one ** step_count)
    corr_two = new_two / (1.0 - beta_two ** step_count)
    new_weight = weight - learn_rate * (corr_one / (jnp.sqrt(corr_two) + adam_eps) + decay_rate * weight)
    return (new_weight, new_one, new_two)

def block_mask(own_flag, prev_flag):
    near_ok = own_flag == 0
    far_ok = jnp.logical_and(near_ok, prev_flag == 0)
    return jnp.concatenate([jnp.broadcast_to(far_ok, (FRAME_TOK,)), jnp.broadcast_to(near_ok, (FRAME_TOK,)), jnp.ones((FRAME_TOK,), bool)])

def window_grad(query_rows, key_window, value_window, grad_rows, allowed):
    scaling = 1.0 / math.sqrt(HEAD_DIM)
    high = lax.Precision.HIGHEST
    query_heads = query_rows.reshape(FRAME_TOK, HEADS, HEAD_DIM).astype(jnp.float32)
    key_heads = key_window.reshape(3 * FRAME_TOK, HEADS, HEAD_DIM).astype(jnp.float32)
    value_heads = value_window.reshape(3 * FRAME_TOK, HEADS, HEAD_DIM).astype(jnp.float32)
    grad_heads = grad_rows.reshape(FRAME_TOK, HEADS, HEAD_DIM).astype(jnp.float32)
    scores = jnp.einsum('qhd,khd->hqk', query_heads, key_heads, precision=high) * scaling
    scores = jnp.where(allowed[None, None, :], scores, -jnp.inf)
    row_max = lax.optimization_barrier(jnp.max(scores, axis=-1, keepdims=True))
    raised = jnp.exp(scores - row_max)
    softmax = raised / lax.optimization_barrier(jnp.sum(raised, axis=-1, keepdims=True))
    dprobs = jnp.einsum('qhd,khd->hqk', grad_heads, value_heads, precision=high)
    row_dot = lax.optimization_barrier(jnp.sum(softmax * dprobs, axis=-1, keepdims=True))
    dscores = (softmax * (dprobs - row_dot) * scaling).astype(jnp.bfloat16)
    window_part = jnp.einsum('hqk,qhd->khd', dscores.astype(jnp.float32), query_heads, precision=high)
    return window_part.reshape(3 * FRAME_TOK, ATT)

def key_gradient(queries, keys_seq, values_seq, grads_seq, flag_seq):
    zero_pad = jnp.zeros((2 * FRAME_TOK, ATT), jnp.bfloat16)
    keys_pad = jnp.concatenate([zero_pad, keys_seq], axis=0)
    values_pad = jnp.concatenate([zero_pad, values_seq], axis=0)
    flag_pad = jnp.concatenate([jnp.ones((1,), jnp.int32), flag_seq.astype(jnp.int32)])

    def one_frame(carry_grad, frame_idx):
        begin = (frame_idx * FRAME_TOK).astype(jnp.int32)
        query_rows = lax.dynamic_slice_in_dim(queries, begin, FRAME_TOK, 0)
        grad_rows = lax.dynamic_slice_in_dim(grads_seq, begin, FRAME_TOK, 0)
        key_window = lax.dynamic_slice_in_dim(keys_pad, begin, 3 * FRAME_TOK, 0)
        value_window = lax.dynamic_slice_in_dim(values_pad, begin, 3 * FRAME_TOK, 0)
        allowed = block_mask(flag_pad[frame_idx + 1], flag_pad[frame_idx])
        window_part = window_grad(query_rows, key_window, value_window, grad_rows, allowed)
        previous = lax.dynamic_slice_in_dim(carry_grad, begin, 3 * FRAME_TOK, 0)
        carry_grad = lax.dynamic_update_slice_in_dim(carry_grad, previous + window_part, begin, 0)
        return (carry_grad, None)
    start_grad = jnp.zeros((TOKENS + 2 * FRAME_TOK, ATT), jnp.float32)
    summed, _ = lax.scan(one_frame, start_grad, jnp.arange(FRAMES, dtype=jnp.int32))
    return summed[2 * FRAME_TOK:].astype(jnp.bfloat16)

def reference(inputs, query_states, key_states, value_states, out_grad, first_flags, weight, moment_one, moment_two):

    def per_seq(accum_grad, seq_idx):
        key_grad = key_gradient(query_states[seq_idx], key_states[seq_idx], value_states[seq_idx], out_grad[seq_idx], first_flags[seq_idx])
        term = lax.dot_general(inputs[seq_idx], key_grad, (((0,), (0,)), ((), ())), preferred_element_type=jnp.float32)
        return (accum_grad + term, None)
    gradient, _ = lax.scan(per_seq, jnp.zeros((DX, ATT), jnp.float32), jnp.arange(SEQS, dtype=jnp.int32))
    return adamw(weight, moment_one, moment_two, gradient)
```

```python
import functools
import math

import jax
import jax.numpy as jnp
from jax import lax
from jax.experimental import pallas as pl
from jax.experimental.pallas import tpu as pltpu
from jax.sharding import Mesh, PartitionSpec as P

HEAD_DIM = 128


beta_one = 0.9
beta_two = 0.95
learn_rate = 0.001
adam_eps = 1e-08
decay_rate = 0.1
step_count = 10.0

TOKENS_BOTH = (((1,), (1,)), ((), ()))
ROWS_BOTH = (((0,), (0,)), ((), ()))


def adamw(weight, moment_one, moment_two, gradient):
    new_one = beta_one * moment_one + (1.0 - beta_one) * gradient
    new_two = beta_two * moment_two + (1.0 - beta_two) * gradient * gradient
    corr_one = new_one / (1.0 - beta_one**step_count)
    corr_two = new_two / (1.0 - beta_two**step_count)
    new_weight = weight - learn_rate * (
        corr_one / (jnp.sqrt(corr_two) + adam_eps) + decay_rate * weight
    )
    return (new_weight, new_one, new_two)


def key_grad_kernel(flags, place, query, grad, key_own, key_near, key_far, val_own, val_near, val_far, out):
    scaling = 1.0 / math.sqrt(HEAD_DIM)
    power = scaling * math.log2(math.e)
    position = place[0]
    near_ok = jnp.logical_and(position >= 1, flags[0, position] == 0)
    far_ok = jnp.logical_and(
        jnp.logical_and(near_ok, position >= 2), flags[0, jnp.maximum(position - 1, 0)] == 0
    )
    queries = query[...]
    grads = grad[...]

    def product(left, right):
        return lax.dot_general(left, right, TOKENS_BOTH, preferred_element_type=jnp.float32)

    keys = (key_far, key_near, key_own)
    values = (val_far, val_near, val_own)
    seen = (far_ok, near_ok, None)
    scores = [product(k[...], queries) for k in keys]
    tops = [jnp.max(s, axis=0, keepdims=True) for s in scores]
    tops = [t if ok is None else jnp.where(ok, t, -jnp.inf) for t, ok in zip(tops, seen)]
    top = functools.reduce(jnp.maximum, tops) * power
    lifts = [top if ok is None else jnp.where(ok, top, jnp.inf) for ok in seen]
    raised = [jnp.exp2(s * power - lift) for s, lift in zip(scores, lifts)]
    total = sum(jnp.sum(r, axis=0, keepdims=True) for r in raised)
    dprobs = [product(v[...], grads) for v in values]
    dots = sum(jnp.sum(r * d, axis=0, keepdims=True) for r, d in zip(raised, dprobs))
    inverse = 1.0 / total
    delta = dots * inverse
    level = inverse * scaling
    for place_of, (r, d) in enumerate(zip(raised, dprobs)):
        dscores = (r * level * (d - delta)).astype(jnp.bfloat16)
        part = jnp.dot(dscores, queries, preferred_element_type=jnp.float32)
        out[place_of] = part.astype(jnp.bfloat16)


def key_grads(flag_row, position, queries, grads, keys, values):
    rows, width = queries.shape
    block = pl.BlockSpec((rows, HEAD_DIM), lambda h: (0, h))
    smem = pl.BlockSpec(memory_space=pltpu.SMEM)
    return pl.pallas_call(
        key_grad_kernel,
        grid=(width // HEAD_DIM,),
        in_specs=[smem, smem] + [block] * 8,
        out_specs=pl.BlockSpec((3, rows, HEAD_DIM), lambda h: (0, 0, h)),
        out_shape=jax.ShapeDtypeStruct((3, rows, width), jnp.bfloat16),
        name="key_grads",
    )(flag_row, position, queries, grads, *keys, *values)


def half_gradient_kernel(which, own, near, far, parts, out):
    half = out.shape[1]
    start = pl.multiple_of(which[0] * half, 128)
    total = None
    for index, features in enumerate((far, near, own)):
        term = lax.dot_general(
            features[...],
            parts[index, :, pl.ds(start, half)],
            ROWS_BOTH,
            preferred_element_type=jnp.float32,
        )
        total = term if total is None else total + term
    out[...] = total.astype(out.dtype)


def half_gradient(which, own, near, far, parts, dtype):
    vmem = pl.BlockSpec(memory_space=pltpu.VMEM)
    return pl.pallas_call(
        half_gradient_kernel,
        in_specs=[pl.BlockSpec(memory_space=pltpu.SMEM)] + [vmem] * 4,
        out_specs=vmem,
        out_shape=jax.ShapeDtypeStruct((own.shape[1], parts.shape[2] // 2), dtype),
        name="half_gradient",
    )(which, own, near, far, parts)


def body(
    inputs,
    query_states,
    key_states,
    value_states,
    out_grad,
    first_flags,
    weight,
    moment_one,
    moment_two,
):
    hops, pairs = lax.axis_size("hop"), lax.axis_size("side")
    sets, cores = lax.axis_size("set"), lax.axis_size("core")
    frames = hops * pairs
    position = lax.axis_index(("hop", "side"))
    core = lax.axis_index("core")
    odd = lax.axis_index("side") == 1

    def behind(value):
        far = lax.ppermute(value, ("hop", "side"), [(i, i + 2) for i in range(frames - 2)])
        near = lax.ppermute(jnp.where(odd, far, value), "side", [(0, 1), (1, 0)])
        return near, far

    keys_own, values_own, features = key_states[0], value_states[0], inputs[0]
    keys_near, keys_far = behind(keys_own)
    values_near, values_far = behind(values_own)
    features_near, features_far = behind(features)
    parts = key_grads(
        first_flags,
        position.reshape(1),
        query_states[0],
        out_grad[0],
        (keys_own, keys_near, keys_far),
        (values_own, values_near, values_far),
    )
    window = (features, features_near, features_far, parts)
    sent = half_gradient((1 - core).reshape(1), *window, jnp.bfloat16)
    taken = lax.ppermute(sent, "core", [(0, 1), (1, 0)])
    kept = half_gradient(core.reshape(1), *window, jnp.float32)
    piece = kept.shape[0] // (frames * sets)
    half = kept.shape[1]
    chip = (kept + taken.astype(jnp.float32)).reshape(hops, pairs, sets, piece, half)
    chip = chip.transpose(2, 1, 0, 3, 4).astype(jnp.bfloat16)
    chip = chip.reshape(sets * pairs, hops, piece, half)
    plane = lax.all_to_all(chip, ("set", "side"), 0, 0)
    plane = jnp.sum(plane.astype(jnp.float32), axis=0).astype(jnp.bfloat16)
    column = lax.all_to_all(plane, "hop", 0, 0)
    mine = jnp.sum(column.astype(jnp.float32), axis=0)
    whole = lax.all_gather(mine, ("set", "core"), axis=0, tiled=False)
    whole = whole.reshape(sets, cores, piece, half).transpose(0, 2, 1, 3)
    gradient = whole.reshape(sets * piece, cores * half)
    return adamw(weight, moment_one, moment_two, gradient)


def solution(mesh):
    clip, frames = mesh.shape["clip"], mesh.shape["tm"]
    grid = Mesh(
        mesh.devices.reshape(clip // 2, 2, frames // 2, 2), ("set", "core", "hop", "side")
    )
    seq, tok = ("set", "core"), ("hop", "side")
    wide = P(seq, tok, None)
    rows = P(tok, None)
    in_specs = (wide,) * 5 + (P(seq, None),) + (rows,) * 3
    return jax.shard_map(
        body, mesh=grid, in_specs=in_specs, out_specs=(rows,) * 3, check_vma=False
    )
```

```python
import functools
import math

import jax
import jax.numpy as jnp
from jax import lax
from jax.experimental import pallas as pl
from jax.experimental.pallas import tpu as pltpu
from jax.sharding import Mesh, PartitionSpec as P


HEAD_DIM = 128


beta_one = 0.9
beta_two = 0.95
learn_rate = 0.001
adam_eps = 1e-08
decay_rate = 0.1
step_count = 10.0

TOKENS_BOTH = (((1,), (1,)), ((), ()))


def adamw(weight, moment_one, moment_two, gradient):
    new_one = beta_one * moment_one + (1.0 - beta_one) * gradient
    new_two = beta_two * moment_two + (1.0 - beta_two) * gradient * gradient
    corr_one = new_one / (1.0 - beta_one**step_count)
    corr_two = new_two / (1.0 - beta_two**step_count)
    new_weight = weight - learn_rate * (
        corr_one / (jnp.sqrt(corr_two) + adam_eps) + decay_rate * weight
    )
    return (new_weight, new_one, new_two)


def near_by(value):
    return pltpu.with_memory_space_constraint(value, pltpu.VMEM)


def key_grad_kernel(flags, place, query, grad, *refs):
    *blocks, out = refs
    count = len(blocks) - 3
    keys, values = blocks[:count], blocks[count:]
    scaling = 1.0 / math.sqrt(HEAD_DIM)
    power = scaling * math.log2(math.e)
    position = place[0]
    near_ok = jnp.logical_and(position >= 1, flags[0, position] == 0)
    far_ok = jnp.logical_and(
        jnp.logical_and(near_ok, position >= 2), flags[0, jnp.maximum(position - 1, 0)] == 0
    )
    queries = query[...]
    grads = grad[...]
    rows = queries.shape[0]

    def product(left, right):
        return lax.dot_general(left, right, TOKENS_BOTH, preferred_element_type=jnp.float32)

    starts = [sum(k.shape[0] for k in keys[:i]) for i in range(count)]
    seen = [(far_ok, near_ok, None)[start // rows] for start in starts]
    scores = [product(k[...], queries) for k in keys]
    tops = [jnp.max(s, axis=0, keepdims=True) for s in scores]
    tops = [t if ok is None else jnp.where(ok, t, -jnp.inf) for t, ok in zip(tops, seen)]
    top = functools.reduce(jnp.maximum, tops) * power
    lifts = [top if ok is None else jnp.where(ok, top, jnp.inf) for ok in seen]
    raised = [jnp.exp2(s * power - lift) for s, lift in zip(scores, lifts)]
    total = sum(jnp.sum(r, axis=0, keepdims=True) for r in raised)
    sliced = [
        values[start // rows][start % rows : start % rows + k.shape[0], :]
        for start, k in zip(starts, keys)
    ]
    dprobs = [product(v, grads) for v in sliced]
    dots = sum(jnp.sum(r * d, axis=0, keepdims=True) for r, d in zip(raised, dprobs))
    inverse = 1.0 / total
    delta = dots * inverse
    level = inverse * scaling
    for start, r, d in zip(starts, raised, dprobs):
        dscores = (r * level * (d - delta)).astype(jnp.bfloat16)
        part = jnp.dot(dscores, queries, preferred_element_type=jnp.float32)
        out[start : start + r.shape[0], :] = part.astype(jnp.bfloat16)


def key_grads(flag_row, position, queries, grads, keys, values):
    rows, width = queries.shape
    smem = pl.BlockSpec(memory_space=pltpu.SMEM)

    def block(array):
        return pl.BlockSpec((array.shape[0], HEAD_DIM), lambda h: (0, h))

    arrays = (queries, grads, *keys, *values)
    return pl.pallas_call(
        key_grad_kernel,
        grid=(width // HEAD_DIM,),
        in_specs=[smem, smem] + [block(a) for a in arrays],
        out_specs=pl.BlockSpec((3 * rows, HEAD_DIM), lambda h: (0, h)),
        out_shape=jax.ShapeDtypeStruct((3 * rows, width), jnp.bfloat16),
        name="key_grads",
    )(flag_row, position, *arrays)


def turn_kernel(value, out):
    out[...] = value[...].T


def turned(value):
    vmem = pl.BlockSpec(memory_space=pltpu.VMEM)
    return pl.pallas_call(
        turn_kernel,
        in_specs=[vmem],
        out_specs=vmem,
        out_shape=jax.ShapeDtypeStruct(value.shape[::-1], value.dtype),
        name="turned",
    )(value)


def gradient_kernel(which, far, near, own, parts, kept, sent):
    half = kept.shape[1]
    rows = near.shape[0]
    turned_near = near[...].T
    for target, side in ((sent, 1 - which[0]), (kept, which[0])):
        start = pl.multiple_of(side * half, 128)
        total = None
        for index, features in enumerate((far[...], turned_near, own[...])):
            term = jnp.dot(
                features,
                parts[index * rows : (index + 1) * rows, pl.ds(start, half)],
                preferred_element_type=jnp.float32,
            )
            total = term if total is None else total + term
        target[...] = total.astype(target.dtype)


def partial_gradient(core, far, near, own, parts):
    vmem = pl.BlockSpec(memory_space=pltpu.VMEM)
    shape = (far.shape[0], parts.shape[1] // 2)
    return pl.pallas_call(
        gradient_kernel,
        in_specs=[pl.BlockSpec(memory_space=pltpu.SMEM)] + [vmem] * 4,
        out_specs=(vmem, vmem),
        out_shape=(
            jax.ShapeDtypeStruct(shape, jnp.float32),
            jax.ShapeDtypeStruct(shape, jnp.bfloat16),
        ),
        name="partial_gradient",
    )(core, far, near, own, parts)


def body(
    inputs,
    query_states,
    key_states,
    value_states,
    out_grad,
    first_flags,
    weight,
    moment_one,
    moment_two,
):
    hops, pairs = lax.axis_size("hop"), lax.axis_size("side")
    sets, cores = lax.axis_size("set"), lax.axis_size("core")
    frames = hops * pairs
    position = lax.axis_index(("hop", "side"))
    core, side = lax.axis_index("core"), lax.axis_index("side")
    swap = [(0, 1), (1, 0)]

    def behind(value):
        far = lax.ppermute(value, ("hop", "side"), [(i, i + 2) for i in range(frames - 2)])
        mixed = jnp.where(side == 1, far, value)
        near = lax.ppermute(mixed, "side", swap)
        return near_by(far), near_by(near)

    keys_own, values_own, features = key_states[0], value_states[0], inputs[0]
    middle = keys_own.shape[0] * 2 // 5
    keys_one = behind(keys_own[:middle])
    keys_two = behind(keys_own[middle:])
    keys_far, keys_near = zip(keys_one, keys_two)
    values_far, values_near = behind(values_own)
    features_far, features_near = behind(features)
    parts = key_grads(
        first_flags,
        position.reshape(1),
        query_states[0],
        out_grad[0],
        (*keys_far, *keys_near, keys_own),
        (values_far, values_near, values_own),
    )
    turned_far, turned_own = turned(features_far), turned(features)
    kept, sent = partial_gradient(
        core.reshape(1), turned_far, features_near, turned_own, parts
    )
    taken = lax.ppermute(sent, "core", swap)
    rows, half = kept.shape[0] // frames, kept.shape[1]
    chip = (kept + taken.astype(jnp.float32)).reshape(hops, pairs, rows, half)
    sent = lax.dynamic_index_in_dim(chip, 1 - side, 1, keepdims=False).astype(jnp.bfloat16)
    kept = lax.dynamic_index_in_dim(chip, side, 1, keepdims=False)
    taken = lax.ppermute(sent, "side", swap)
    line = (kept + taken.astype(jnp.float32)).astype(jnp.bfloat16)
    column = lax.all_to_all(line, "hop", 0, 0)
    mine = jnp.sum(column.astype(jnp.float32), axis=0).astype(jnp.bfloat16)
    whole = lax.all_gather(mine, ("set", "core"), axis=0, tiled=False)
    whole = jnp.sum(whole.astype(jnp.float32).reshape(sets, cores, rows, half), axis=0)
    gradient = whole.transpose(1, 0, 2).reshape(rows, cores * half)
    return adamw(weight, moment_one, moment_two, gradient)


def solution(mesh):
    clip, frames = mesh.shape["clip"], mesh.shape["tm"]
    grid = Mesh(
        mesh.devices.reshape(clip // 2, 2, frames // 2, 2), ("set", "core", "hop", "side")
    )
    seq, tok = ("set", "core"), ("hop", "side")
    wide = P(seq, tok, None)
    rows = P(tok, None)
    in_specs = (wide,) * 5 + (P(seq, None),) + (rows,) * 3

    return jax.shard_map(body, mesh=grid, in_specs=in_specs, out_specs=(rows,) * 3, check_vma=False)
```

```python
import functools
import math

import jax
import jax.numpy as jnp
from jax import lax
from jax.experimental import pallas as pl
from jax.experimental.pallas import tpu as pltpu
from jax.sharding import Mesh, PartitionSpec as P


HEAD_DIM = 128


beta_one = 0.9
beta_two = 0.95
learn_rate = 0.001
adam_eps = 1e-08
decay_rate = 0.1
step_count = 10.0

TOKENS_BOTH = (((1,), (1,)), ((), ()))


def adamw(weight, moment_one, moment_two, gradient):
    new_one = beta_one * moment_one + (1.0 - beta_one) * gradient
    new_two = beta_two * moment_two + (1.0 - beta_two) * gradient * gradient
    corr_one = new_one / (1.0 - beta_one**step_count)
    corr_two = new_two / (1.0 - beta_two**step_count)
    new_weight = weight - learn_rate * (
        corr_one / (jnp.sqrt(corr_two) + adam_eps) + decay_rate * weight
    )
    return (new_weight, new_one, new_two)


def near_by(value):
    return pltpu.with_memory_space_constraint(value, pltpu.VMEM)


def folded(value):
    return value.reshape(value.shape[0] // 8, 8, value.shape[1])


def head_columns(refs, head):
    columns = slice(head * HEAD_DIM, (head + 1) * HEAD_DIM)
    parts = [ref[:, columns] for ref in refs]
    return parts[0] if len(parts) == 1 else jnp.concatenate(parts, axis=0)


def key_grads_kernel(key_cuts, val_cuts, flags, place, query, grad, *refs):
    keys, refs = refs[:key_cuts], refs[key_cuts:]
    values, refs = refs[:val_cuts], refs[val_cuts:]
    out, *scratch = refs
    scores, dprobs, raiseds, dscores = (scratch[i : i + 2] for i in (0, 2, 4, 6))
    rows, width = query.shape
    heads = width // HEAD_DIM
    lanes = scores[0].shape[1]
    scaling = 1.0 / math.sqrt(HEAD_DIM)
    power = scaling * math.log2(math.e)
    position = place[0]
    near_ok = jnp.logical_and(position >= 1, flags[0, position] == 0)
    far_ok = jnp.logical_and(
        jnp.logical_and(near_ok, position >= 2), flags[0, jnp.maximum(position - 1, 0)] == 0
    )
    seen = (None, far_ok, near_ok)
    blank = jnp.zeros((lanes - rows, HEAD_DIM), query.dtype)
    step = 32 if rows % 32 == 0 else rows
    base = pl.multiple_of(jnp.minimum(position, 0) * 32, 32)

    def piece_of(start, size=step):
        return pl.ds(base + start, size)

    def padded(ref, head):
        return jnp.concatenate([head_columns([ref], head), blank], axis=0)

    def products(head):
        slot = head % 2
        for refs_of, other, target in ((keys, query, scores), (values, grad, dprobs)):
            target[slot][piece_of(0, 3 * rows), :] = lax.dot_general(
                head_columns(refs_of, head),
                padded(other, head),
                TOKENS_BOTH,
                preferred_element_type=jnp.float32,
            )

    def softmax(head):
        slot = head % 2
        tops = []
        for frame, ok in enumerate(seen):
            top = jnp.max(folded(scores[slot][piece_of(frame * rows, rows), :]), axis=0)
            tops.append(top if ok is None else jnp.where(ok, top, -jnp.inf))
        top = jnp.max(functools.reduce(jnp.maximum, tops), axis=0, keepdims=True) * power
        total = dots = 0.0
        for frame, ok in enumerate(seen):
            lift = top if ok is None else jnp.where(ok, top, jnp.inf)
            for start in range(frame * rows, (frame + 1) * rows, step):
                piece = piece_of(start)
                raised = jnp.exp2(scores[slot][piece, :] * power - lift)
                raiseds[slot][piece, :] = raised
                total = total + jnp.sum(folded(raised), axis=0)
                dots = dots + jnp.sum(folded(raised * dprobs[slot][piece, :]), axis=0)
        inverse = 1.0 / jnp.sum(total, axis=0, keepdims=True)
        delta = jnp.sum(dots, axis=0, keepdims=True) * inverse
        level = inverse * scaling
        for start in range(0, 3 * rows, step):
            piece = piece_of(start)
            value = raiseds[slot][piece, :] * level * (dprobs[slot][piece, :] - delta)
            dscores[slot][piece, :] = value.astype(dscores[slot].dtype)

    def collect(head):
        part = jnp.dot(
            dscores[head % 2][piece_of(0, 3 * rows), :],
            padded(query, head),
            preferred_element_type=jnp.float32,
        )
        out[:, head * HEAD_DIM : (head + 1) * HEAD_DIM] = part.astype(out.dtype)

    for beat in range(heads + 2):
        if beat >= 2:
            collect(beat - 2)
        if beat < heads:
            products(beat)
        if 1 <= beat <= heads:
            softmax(beat - 1)


def key_grads(flag_row, position, queries, grads, keys, values):
    rows, width = queries.shape
    lanes = pl.cdiv(rows, 128) * 128
    smem = pl.BlockSpec(memory_space=pltpu.SMEM)
    vmem = pl.BlockSpec(memory_space=pltpu.VMEM)
    arrays = [near_by(a) for a in (queries, grads, *keys, *values)]
    return pl.pallas_call(
        functools.partial(key_grads_kernel, len(keys), len(values)),
        in_specs=[smem, smem] + [vmem] * len(arrays),
        out_specs=vmem,
        out_shape=pltpu.VMEM((3 * rows, width), jnp.bfloat16),
        scratch_shapes=[
            pltpu.VMEM((3 * rows, lanes), dtype)
            for dtype in (jnp.float32, jnp.float32, jnp.float32, jnp.bfloat16)
            for _ in range(2)
        ],
        compiler_params=pltpu.CompilerParams(vmem_limit_bytes=24 << 20),
        name="key_grads",
    )(flag_row, position, *arrays)


def turn_kernel(*refs):
    *values, out = refs
    out[...] = jnp.concatenate([v[...] for v in values], axis=0).T


def turned(*values):
    vmem = pl.BlockSpec(memory_space=pltpu.VMEM)
    tokens = sum(v.shape[0] for v in values)
    return pl.pallas_call(
        turn_kernel,
        in_specs=[vmem] * len(values),
        out_specs=vmem,
        out_shape=pltpu.VMEM((values[0].shape[1], tokens), values[0].dtype),
        compiler_params=pltpu.CompilerParams(vmem_limit_bytes=16 << 20),
        name="turned",
    )(*[near_by(v) for v in values])


def gradient_kernel(which, early, late, parts, kept, sent, whole):
    half = kept.shape[1]
    features = jnp.concatenate([early[...], late[...].T], axis=1)
    whole[...] = jnp.dot(features, parts[...], preferred_element_type=jnp.float32)
    for target, side in ((sent, 1 - which[0]), (kept, which[0])):
        start = pl.multiple_of(side * half, 128)
        target[...] = whole[:, pl.ds(start, half)].astype(target.dtype)


def partial_gradient(core, early, late, parts):
    vmem = pl.BlockSpec(memory_space=pltpu.VMEM)
    width = parts.shape[1]
    shape = (early.shape[0], width // 2)
    return pl.pallas_call(
        gradient_kernel,
        in_specs=[pl.BlockSpec(memory_space=pltpu.SMEM)] + [vmem] * 3,
        out_specs=(vmem, vmem),
        out_shape=(pltpu.VMEM(shape, jnp.float32), pltpu.VMEM(shape, jnp.bfloat16)),
        scratch_shapes=[pltpu.VMEM((early.shape[0], width), jnp.float32)],
        compiler_params=pltpu.CompilerParams(vmem_limit_bytes=24 << 20),
        name="partial_gradient",
    )(core, *[near_by(a) for a in (early, late, parts)])


def body(
    inputs,
    query_states,
    key_states,
    value_states,
    out_grad,
    first_flags,
    weight,
    moment_one,
    moment_two,
):
    hops, pairs = lax.axis_size("hop"), lax.axis_size("side")
    sets, cores = lax.axis_size("set"), lax.axis_size("core")
    frames = hops * pairs
    position = lax.axis_index(("hop", "side"))
    core, side = lax.axis_index("core"), lax.axis_index("side")
    swap = [(0, 1), (1, 0)]

    def behind(value):
        far = lax.ppermute(value, ("hop", "side"), [(i, i + 2) for i in range(frames - 2)])
        mixed = jnp.where(side == 1, far, value)
        near = lax.ppermute(mixed, "side", swap)
        return far, near

    keys_own, values_own, features = key_states[0], value_states[0], inputs[0]
    middle = keys_own.shape[0] * 2 // 5
    keys_one = behind(keys_own[:middle])
    keys_two = behind(keys_own[middle:])
    keys_far, keys_near = zip(keys_one, keys_two)
    values_far, values_near = behind(values_own)
    features_far, features_near = behind(features)
    parts = key_grads(
        first_flags,
        position.reshape(1),
        query_states[0],
        out_grad[0],
        (keys_own, *keys_far, *keys_near),
        (values_own, values_far, values_near),
    )
    early = turned(features, features_far)
    kept, sent = partial_gradient(core.reshape(1), early, features_near, parts)
    taken = lax.ppermute(sent, "core", swap)
    rows, half = kept.shape[0] // frames, kept.shape[1]
    chip = (kept + taken.astype(jnp.float32)).reshape(hops, pairs, rows, half)
    sent = lax.dynamic_index_in_dim(chip, 1 - side, 1, keepdims=False).astype(jnp.bfloat16)
    kept = lax.dynamic_index_in_dim(chip, side, 1, keepdims=False)
    taken = lax.ppermute(sent, "side", swap)
    line = (kept + taken.astype(jnp.float32)).astype(jnp.bfloat16)
    column = lax.all_to_all(line, "hop", 0, 0)
    mine = jnp.sum(column.astype(jnp.float32), axis=0).astype(jnp.bfloat16)
    whole = lax.all_gather(mine, ("set", "core"), axis=0, tiled=False)
    whole = jnp.sum(whole.astype(jnp.float32).reshape(sets, cores, rows, half), axis=0)
    gradient = whole.transpose(1, 0, 2).reshape(rows, cores * half)
    return adamw(weight, moment_one, moment_two, gradient)


def solution(mesh):
    clip, frames = mesh.shape["clip"], mesh.shape["tm"]
    grid = Mesh(
        mesh.devices.reshape(clip // 2, 2, frames // 2, 2), ("set", "core", "hop", "side")
    )
    seq, tok = ("set", "core"), ("hop", "side")
    wide = P(seq, tok, None)
    rows = P(tok, None)
    in_specs = (wide,) * 5 + (P(seq, None),) + (rows,) * 3

    return jax.shard_map(body, mesh=grid, in_specs=in_specs, out_specs=(rows,) * 3, check_vma=False)
```

```python
import functools
import math

import jax
import jax.numpy as jnp
from jax import lax
from jax.experimental import pallas as pl
from jax.experimental.pallas import tpu as pltpu
from jax.sharding import Mesh, PartitionSpec as P


HEAD_DIM = 128


beta_one = 0.9
beta_two = 0.95
learn_rate = 0.001
adam_eps = 1e-08
decay_rate = 0.1
step_count = 10.0

TOKENS_BOTH = (((1,), (1,)), ((), ()))


def adamw(weight, moment_one, moment_two, gradient):
    new_one = beta_one * moment_one + (1.0 - beta_one) * gradient
    new_two = beta_two * moment_two + (1.0 - beta_two) * gradient * gradient
    corr_one = new_one / (1.0 - beta_one**step_count)
    corr_two = new_two / (1.0 - beta_two**step_count)
    new_weight = weight - learn_rate * (
        corr_one / (jnp.sqrt(corr_two) + adam_eps) + decay_rate * weight
    )
    return (new_weight, new_one, new_two)


def near_by(value):
    return pltpu.with_memory_space_constraint(value, pltpu.VMEM)


def far_off(value):
    return pltpu.with_memory_space_constraint(value, pltpu.HBM)


def cut_kernel(spans, *refs):
    wholes, outs, sem = refs[: len(spans)], refs[len(spans) : -1], refs[-1]
    copies, index = [], 0
    for whole, rows in zip(wholes, spans):
        for start, size in rows:
            copies.append(
                pltpu.make_async_copy(whole.at[pl.ds(start, size)], outs[index], sem.at[index])
            )
            index += 1
    for copy in copies:
        copy.start()
    for copy in copies:
        copy.wait()


def cut_out(wholes, spans):
    anywhere = pl.BlockSpec(memory_space=pl.ANY)
    shapes = [
        jax.ShapeDtypeStruct((size, whole.shape[1]), whole.dtype)
        for whole, rows in zip(wholes, spans)
        for _, size in rows
    ]
    return pl.pallas_call(
        functools.partial(cut_kernel, spans),
        in_specs=[anywhere] * len(wholes),
        out_specs=[pl.BlockSpec(memory_space=pltpu.VMEM)] * len(shapes),
        out_shape=shapes,
        scratch_shapes=[pltpu.SemaphoreType.DMA((len(shapes),))],
        compiler_params=pltpu.CompilerParams(vmem_limit_bytes=4 << 20),
        name="cut_out",
    )(*[far_off(whole) for whole in wholes])


def pick_kernel(start, far, whole, out, sem):
    side = lax.axis_index("side")

    @pl.when(side == 1)
    def _():
        copy = pltpu.make_async_copy(far, out, sem)
        copy.start()
        copy.wait()

    @pl.when(side != 1)
    def _():
        copy = pltpu.make_async_copy(whole.at[pl.ds(start, out.shape[0])], out, sem)
        copy.start()
        copy.wait()


def picked(far, whole, start):
    anywhere = pl.BlockSpec(memory_space=pl.ANY)
    return pl.pallas_call(
        functools.partial(pick_kernel, start),
        in_specs=[anywhere, anywhere],
        out_specs=pl.BlockSpec(memory_space=pltpu.VMEM),
        out_shape=jax.ShapeDtypeStruct(far.shape, far.dtype),
        scratch_shapes=[pltpu.SemaphoreType.DMA],
        compiler_params=pltpu.CompilerParams(vmem_limit_bytes=1 << 20),
        name="picked",
    )(far, far_off(whole))


def frame_index():
    return lax.axis_index("hop") * lax.axis_size("side") + lax.axis_index("side")


def folded(value):
    return value.reshape(value.shape[0] // 8, 8, value.shape[1])


def head_columns(refs, head):
    columns = slice(head * HEAD_DIM, (head + 1) * HEAD_DIM)
    parts = [ref[:, columns] for ref in refs]
    return parts[0] if len(parts) == 1 else jnp.concatenate(parts, axis=0)


def key_grads_kernel(key_cuts, val_cuts, flags, query, grad, *refs):
    keys, refs = refs[:key_cuts], refs[key_cuts:]
    values, refs = refs[:val_cuts], refs[val_cuts:]
    out, *scratch = refs
    scores, dprobs, raiseds, dscores = (scratch[i : i + 2] for i in (0, 2, 4, 6))
    rows, width = query.shape
    heads = width // HEAD_DIM
    lanes = scores[0].shape[1]
    scaling = 1.0 / math.sqrt(HEAD_DIM)
    power = scaling * math.log2(math.e)
    position = frame_index()
    near_ok = jnp.logical_and(position >= 1, flags[0, position] == 0)
    far_ok = jnp.logical_and(
        jnp.logical_and(near_ok, position >= 2), flags[0, jnp.maximum(position - 1, 0)] == 0
    )
    seen = (None, far_ok, near_ok)
    blank = jnp.zeros((lanes - rows, HEAD_DIM), query.dtype)
    step = 32 if rows % 32 == 0 else rows
    base = pl.multiple_of(jnp.minimum(flags[0, 0], 0) * 32, 32)

    def piece_of(start, size=step):
        return pl.ds(base + start, size)

    def padded(ref, head):
        return jnp.concatenate([head_columns([ref], head), blank], axis=0)

    def products(head):
        slot = head % 2
        for refs_of, other, target in ((keys, query, scores), (values, grad, dprobs)):
            target[slot][piece_of(0, 3 * rows), :] = lax.dot_general(
                head_columns(refs_of, head),
                padded(other, head),
                TOKENS_BOTH,
                preferred_element_type=jnp.float32,
            )

    def softmax(head):
        slot = head % 2
        tops = []
        for frame, ok in enumerate(seen):
            top = jnp.max(folded(scores[slot][piece_of(frame * rows, rows), :]), axis=0)
            tops.append(top if ok is None else jnp.where(ok, top, -jnp.inf))
        top = jnp.max(functools.reduce(jnp.maximum, tops), axis=0, keepdims=True) * power
        total = dots = 0.0
        for frame, ok in enumerate(seen):
            lift = top if ok is None else jnp.where(ok, top, jnp.inf)
            for start in range(frame * rows, (frame + 1) * rows, step):
                piece = piece_of(start)
                raised = jnp.exp2(scores[slot][piece, :] * power - lift)
                raiseds[slot][piece, :] = raised
                total = total + jnp.sum(folded(raised), axis=0)
                dots = dots + jnp.sum(folded(raised * dprobs[slot][piece, :]), axis=0)
        inverse = 1.0 / jnp.sum(total, axis=0, keepdims=True)
        delta = jnp.sum(dots, axis=0, keepdims=True) * inverse
        level = inverse * scaling
        for start in range(0, 3 * rows, step):
            piece = piece_of(start)
            value = raiseds[slot][piece, :] * level * (dprobs[slot][piece, :] - delta)
            dscores[slot][piece, :] = value.astype(dscores[slot].dtype)

    def collect(head):
        part = jnp.dot(
            dscores[head % 2][piece_of(0, 3 * rows), :],
            padded(query, head),
            preferred_element_type=jnp.float32,
        )
        out[:, head * HEAD_DIM : (head + 1) * HEAD_DIM] = part.astype(out.dtype)

    for beat in range(heads + 2):
        if beat >= 2:
            collect(beat - 2)
        if beat < heads:
            products(beat)
        if 1 <= beat <= heads:
            softmax(beat - 1)


def key_grads(flag_row, queries, grads, keys, values):
    rows, width = queries.shape
    lanes = pl.cdiv(rows, 128) * 128
    smem = pl.BlockSpec(memory_space=pltpu.SMEM)
    vmem = pl.BlockSpec(memory_space=pltpu.VMEM)
    arrays = [near_by(a) for a in (queries, grads, *keys, *values)]
    return pl.pallas_call(
        functools.partial(key_grads_kernel, len(keys), len(values)),
        in_specs=[smem] + [vmem] * len(arrays),
        out_specs=vmem,
        out_shape=pltpu.VMEM((3 * rows, width), jnp.bfloat16),
        scratch_shapes=[
            pltpu.VMEM((3 * rows, lanes), dtype)
            for dtype in (jnp.float32, jnp.float32, jnp.float32, jnp.bfloat16)
            for _ in range(2)
        ],
        compiler_params=pltpu.CompilerParams(vmem_limit_bytes=24 << 20),
        name="key_grads",
    )(flag_row, *arrays)


def turn_kernel(*refs):
    *values, out = refs
    out[...] = jnp.concatenate([v[...] for v in values], axis=0).T


def turned(*values):
    vmem = pl.BlockSpec(memory_space=pltpu.VMEM)
    tokens = sum(v.shape[0] for v in values)
    return pl.pallas_call(
        turn_kernel,
        in_specs=[vmem] * len(values),
        out_specs=vmem,
        out_shape=pltpu.VMEM((values[0].shape[1], tokens), values[0].dtype),
        compiler_params=pltpu.CompilerParams(vmem_limit_bytes=16 << 20),
        name="turned",
    )(*[near_by(v) for v in values])


def gradient_kernel(early, parts, *refs):
    *late, kept, sent, whole = refs
    half = kept.shape[1]
    last = jnp.concatenate([ref[...] for ref in late], axis=0).T
    features = jnp.concatenate([early[...], last], axis=1)
    whole[...] = jnp.dot(features, parts[...], preferred_element_type=jnp.float32)
    core = lax.axis_index("core")
    for target, side in ((sent, 1 - core), (kept, core)):
        start = pl.multiple_of(side * half, 128)
        target[...] = whole[:, pl.ds(start, half)].astype(target.dtype)


def partial_gradient(early, late, parts):
    vmem = pl.BlockSpec(memory_space=pltpu.VMEM)
    width = parts.shape[1]
    shape = (early.shape[0], width // 2)
    return pl.pallas_call(
        gradient_kernel,
        in_specs=[vmem] * (2 + len(late)),
        out_specs=(vmem, vmem),
        out_shape=(pltpu.VMEM(shape, jnp.float32), pltpu.VMEM(shape, jnp.bfloat16)),
        scratch_shapes=[pltpu.VMEM((early.shape[0], width), jnp.float32)],
        compiler_params=pltpu.CompilerParams(vmem_limit_bytes=24 << 20),
        name="partial_gradient",
    )(*[near_by(a) for a in (early, parts, *late)])


def body(
    inputs,
    query_states,
    key_states,
    value_states,
    out_grad,
    first_flags,
    weight,
    moment_one,
    moment_two,
):
    hops, pairs = lax.axis_size("hop"), lax.axis_size("side")
    frames = hops * pairs
    swap = [(0, 1), (1, 0)]

    own = (key_states[0], value_states[0], inputs[0])
    tokens = own[0].shape[0]
    cut = tokens * 9 // 20 // 16 * 16
    spans = ((0, cut), (cut, tokens - cut))
    first = cut_out(own[:1], (spans[:1],))
    pieces = [*first, *cut_out(own, (spans[1:], spans, spans))]

    def behind(value, index):
        far = lax.ppermute(value, ("hop", "side"), [(i, i + 2) for i in range(frames - 2)])
        mixed = picked(far, own[index // 2], spans[index % 2][0])
        near = lax.ppermute(mixed, "side", swap)
        return far, near

    moved = [behind(piece, index) for index, piece in enumerate(pieces)]
    keys, values, features = (
        (whole, *zip(*moved[2 * i : 2 * i + 2])) for i, whole in enumerate(own)
    )
    early = turned(features[0], *features[1])
    parts = key_grads(
        first_flags,
        query_states[0],
        out_grad[0],
        (keys[0], *keys[1], *keys[2]),
        (values[0], *values[1], *values[2]),
    )
    kept, sent = partial_gradient(early, features[2], parts)
    taken = lax.ppermute(sent, "core", swap)
    rows, half = kept.shape[0] // frames, kept.shape[1]
    blocks = (hops, pairs, rows, half)
    kept, sent = by_side(kept.reshape(blocks), taken.reshape(blocks))
    taken = lax.ppermute(sent, "side", swap)
    mine = over_hops(kept, taken)
    return updated(*over_clip(mine, swap), weight, moment_one, moment_two)


def small_call(kernel, *arrays, out):
    vmem = pl.BlockSpec(memory_space=pltpu.VMEM)
    return pl.pallas_call(
        kernel,
        in_specs=[vmem] * len(arrays),
        out_specs=jax.tree.map(lambda _: vmem, out),
        out_shape=out,
        compiler_params=pltpu.CompilerParams(vmem_limit_bytes=16 << 20),
    )(*arrays)


def wide(shape):
    return jax.ShapeDtypeStruct(shape, jnp.float32)


def thin(shape):
    return jax.ShapeDtypeStruct(shape, jnp.bfloat16)


def by_side_kernel(kept, taken, stay, leave):
    side = lax.axis_index("side")
    leave[...] = (kept[:, 1 - side] + taken[:, 1 - side].astype(jnp.float32)).astype(leave.dtype)
    stay[...] = kept[:, side] + taken[:, side].astype(jnp.float32)


def by_side(kept, taken):
    hops, _, rows, half = kept.shape
    shape = (hops, rows, half)
    return small_call(by_side_kernel, kept, taken, out=(wide(shape), thin(shape)))


def by_hop_kernel(steps, kept, taken, stay, *leave):
    place, hops = lax.axis_index("hop"), kept.shape[0]
    for step, out in zip((0, *steps), (stay, *leave)):
        block = (place + step) % hops
        out[...] = (kept[block] + taken[block].astype(jnp.float32)).astype(out.dtype)


def add_kernel(first, *refs):
    *others, out = refs
    total = first[...].astype(jnp.float32)
    for other in others:
        total = total + other[...].astype(jnp.float32)
    out[...] = total.astype(out.dtype)


def over_hops(kept, taken):
    hops, rows, half = kept.shape
    if hops > 4:
        line = small_call(add_kernel, kept, taken, out=thin(kept.shape))
        column = lax.all_to_all(line, "hop", 0, 0)
        return small_call(add_kernel, *column, out=thin((rows, half)))
    steps = sorted(range(1, hops), key=lambda k: -min(k, hops - k))
    stay, *leave = small_call(
        functools.partial(by_hop_kernel, steps),
        kept,
        taken,
        out=(wide((rows, half)), *[thin((rows, half))] * len(steps)),
    )
    come = [
        lax.ppermute(block, "hop", [(i, (i + step) % hops) for i in range(hops)])
        for step, block in zip(steps, leave)
    ]
    return small_call(add_kernel, stay, *come, out=thin((rows, half)))


def over_clip(mine, swap):
    sets = lax.axis_size("set")
    if sets == 2:
        terms = (mine, lax.ppermute(mine, "set", swap))
    else:
        terms = tuple(lax.all_gather(mine, "set", axis=0, tiled=False))
    total = small_call(add_kernel, *terms, out=wide(mine.shape))
    return total, lax.ppermute(total, "core", swap)


def update_kernel(own, other, weight, moment_one, moment_two, *outs):
    half = own.shape[1]
    core = lax.axis_index("core")
    for side, part in ((core, own), (1 - core, other)):
        columns = pl.ds(pl.multiple_of(side * half, 128), half)
        olds = (ref[:, columns] for ref in (weight, moment_one, moment_two))
        for out, new in zip(outs, adamw(*olds, part[...])):
            out[:, columns] = new


def updated(own, other, *state):
    return small_call(update_kernel, own, other, *state, out=(wide(state[0].shape),) * 3)


def solution(mesh):
    clip, frames = mesh.shape["clip"], mesh.shape["tm"]
    grid = Mesh(
        mesh.devices.reshape(clip // 2, 2, frames // 2, 2), ("set", "core", "hop", "side")
    )
    seq, tok = ("set", "core"), ("hop", "side")
    wide = P(seq, tok, None)
    rows = P(tok, None)
    in_specs = (wide,) * 5 + (P(seq, None),) + (rows,) * 3

    return jax.shard_map(body, mesh=grid, in_specs=in_specs, out_specs=(rows,) * 3, check_vma=False)
```

```python
import functools
import math

import jax
import jax.numpy as jnp
from jax import lax
from jax.experimental import pallas as pl
from jax.experimental.pallas import tpu as pltpu
from jax.sharding import Mesh, PartitionSpec as P


HEAD_DIM = 128


beta_one = 0.9
beta_two = 0.95
learn_rate = 0.001
adam_eps = 1e-08
decay_rate = 0.1
step_count = 10.0

TOKENS_BOTH = (((1,), (1,)), ((), ()))


def adamw(weight, moment_one, moment_two, gradient):
    new_one = beta_one * moment_one + (1.0 - beta_one) * gradient
    new_two = beta_two * moment_two + (1.0 - beta_two) * gradient * gradient
    corr_one = new_one / (1.0 - beta_one**step_count)
    corr_two = new_two / (1.0 - beta_two**step_count)
    new_weight = weight - learn_rate * (
        corr_one / (jnp.sqrt(corr_two) + adam_eps) + decay_rate * weight
    )
    return (new_weight, new_one, new_two)


def near_by(value):
    return pltpu.with_memory_space_constraint(value, pltpu.VMEM)


def far_off(value):
    return pltpu.with_memory_space_constraint(value, pltpu.HBM)


def cut_kernel(spans, *refs):
    wholes, outs, sem = refs[: len(spans)], refs[len(spans) : -1], refs[-1]
    copies, index = [], 0
    for whole, rows in zip(wholes, spans):
        for start, size in rows:
            copies.append(
                pltpu.make_async_copy(whole.at[pl.ds(start, size)], outs[index], sem.at[index])
            )
            index += 1
    for copy in copies:
        copy.start()
    for copy in copies:
        copy.wait()


def cut_out(wholes, spans):
    anywhere = pl.BlockSpec(memory_space=pl.ANY)
    shapes = [
        jax.ShapeDtypeStruct((size, whole.shape[1]), whole.dtype)
        for whole, rows in zip(wholes, spans)
        for _, size in rows
    ]
    return pl.pallas_call(
        functools.partial(cut_kernel, spans),
        in_specs=[anywhere] * len(wholes),
        out_specs=[pl.BlockSpec(memory_space=pltpu.VMEM)] * len(shapes),
        out_shape=shapes,
        scratch_shapes=[pltpu.SemaphoreType.DMA((len(shapes),))],
        compiler_params=pltpu.CompilerParams(vmem_limit_bytes=4 << 20),
        name="cut_out",
    )(*[far_off(whole) for whole in wholes])


def pick_kernel(start, far, whole, out, sem):
    side = lax.axis_index("side")

    @pl.when(side == 1)
    def _():
        copy = pltpu.make_async_copy(far, out, sem)
        copy.start()
        copy.wait()

    @pl.when(side != 1)
    def _():
        copy = pltpu.make_async_copy(whole.at[pl.ds(start, out.shape[0])], out, sem)
        copy.start()
        copy.wait()


def picked(far, whole, start):
    anywhere = pl.BlockSpec(memory_space=pl.ANY)
    return pl.pallas_call(
        functools.partial(pick_kernel, start),
        in_specs=[anywhere, anywhere],
        out_specs=pl.BlockSpec(memory_space=pltpu.VMEM),
        out_shape=jax.ShapeDtypeStruct(far.shape, far.dtype),
        scratch_shapes=[pltpu.SemaphoreType.DMA],
        compiler_params=pltpu.CompilerParams(vmem_limit_bytes=1 << 20),
        name="picked",
    )(far, far_off(whole))


def frame_index():
    return lax.axis_index("hop") * lax.axis_size("side") + lax.axis_index("side")


def folded(value):
    return value.reshape(value.shape[0] // 8, 8, value.shape[1])


def head_columns(refs, head):
    columns = slice(head * HEAD_DIM, (head + 1) * HEAD_DIM)
    parts = [ref[:, columns] for ref in refs]
    return parts[0] if len(parts) == 1 else jnp.concatenate(parts, axis=0)


def key_grads_kernel(key_cuts, val_cuts, flags, query, grad, *refs):
    keys, refs = refs[:key_cuts], refs[key_cuts:]
    values, refs = refs[:val_cuts], refs[val_cuts:]
    out, *scratch = refs
    scores, dprobs, raiseds, dscores = (scratch[i : i + 2] for i in (0, 2, 4, 6))
    rows, width = query.shape
    heads = width // HEAD_DIM
    lanes = scores[0].shape[1]
    scaling = 1.0 / math.sqrt(HEAD_DIM)
    power = scaling * math.log2(math.e)
    position = frame_index()
    near_ok = jnp.logical_and(position >= 1, flags[0, position] == 0)
    far_ok = jnp.logical_and(
        jnp.logical_and(near_ok, position >= 2), flags[0, jnp.maximum(position - 1, 0)] == 0
    )
    seen = (None, far_ok, near_ok)
    blank = jnp.zeros((lanes - rows, HEAD_DIM), query.dtype)
    step = 32 if rows % 32 == 0 else rows
    base = pl.multiple_of(jnp.minimum(flags[0, 0], 0) * 32, 32)

    def piece_of(start, size=step):
        return pl.ds(base + start, size)

    def padded(ref, head):
        return jnp.concatenate([head_columns([ref], head), blank], axis=0)

    def products(head):
        slot = head % 2
        for refs_of, other, target in ((keys, query, scores), (values, grad, dprobs)):
            target[slot][piece_of(0, 3 * rows), :] = lax.dot_general(
                head_columns(refs_of, head),
                padded(other, head),
                TOKENS_BOTH,
                preferred_element_type=jnp.float32,
            )

    def softmax(head):
        slot = head % 2
        tops = []
        for frame, ok in enumerate(seen):
            top = jnp.max(folded(scores[slot][piece_of(frame * rows, rows), :]), axis=0)
            tops.append(top if ok is None else jnp.where(ok, top, -jnp.inf))
        top = jnp.max(functools.reduce(jnp.maximum, tops), axis=0, keepdims=True) * power
        total = dots = 0.0
        for frame, ok in enumerate(seen):
            lift = top if ok is None else jnp.where(ok, top, jnp.inf)
            for start in range(frame * rows, (frame + 1) * rows, step):
                piece = piece_of(start)
                raised = jnp.exp2(scores[slot][piece, :] * power - lift)
                raiseds[slot][piece, :] = raised
                total = total + jnp.sum(folded(raised), axis=0)
                dots = dots + jnp.sum(folded(raised * dprobs[slot][piece, :]), axis=0)
        inverse = 1.0 / jnp.sum(total, axis=0, keepdims=True)
        delta = jnp.sum(dots, axis=0, keepdims=True) * inverse
        level = inverse * scaling
        for start in range(0, 3 * rows, step):
            piece = piece_of(start)
            value = raiseds[slot][piece, :] * level * (dprobs[slot][piece, :] - delta)
            dscores[slot][piece, :] = value.astype(dscores[slot].dtype)

    def collect(head):
        part = jnp.dot(
            dscores[head % 2][piece_of(0, 3 * rows), :],
            padded(query, head),
            preferred_element_type=jnp.float32,
        )
        out[:, head * HEAD_DIM : (head + 1) * HEAD_DIM] = part.astype(out.dtype)

    for beat in range(heads + 2):
        if beat >= 2:
            collect(beat - 2)
        if beat < heads:
            products(beat)
        if 1 <= beat <= heads:
            softmax(beat - 1)


def key_grads(flag_row, queries, grads, keys, values):
    rows, width = queries.shape
    lanes = pl.cdiv(rows, 128) * 128
    smem = pl.BlockSpec(memory_space=pltpu.SMEM)
    vmem = pl.BlockSpec(memory_space=pltpu.VMEM)
    arrays = [near_by(a) for a in (queries, grads, *keys, *values)]
    return pl.pallas_call(
        functools.partial(key_grads_kernel, len(keys), len(values)),
        in_specs=[smem] + [vmem] * len(arrays),
        out_specs=vmem,
        out_shape=pltpu.VMEM((3 * rows, width), jnp.bfloat16),
        scratch_shapes=[
            pltpu.VMEM((3 * rows, lanes), dtype)
            for dtype in (jnp.float32, jnp.float32, jnp.float32, jnp.bfloat16)
            for _ in range(2)
        ],
        compiler_params=pltpu.CompilerParams(vmem_limit_bytes=24 << 20),
        name="key_grads",
    )(flag_row, *arrays)


def turn_kernel(*refs):
    *values, out = refs
    out[...] = jnp.concatenate([v[...] for v in values], axis=0).T


def turned(*values):
    vmem = pl.BlockSpec(memory_space=pltpu.VMEM)
    tokens = sum(v.shape[0] for v in values)
    return pl.pallas_call(
        turn_kernel,
        in_specs=[vmem] * len(values),
        out_specs=vmem,
        out_shape=pltpu.VMEM((values[0].shape[1], tokens), values[0].dtype),
        compiler_params=pltpu.CompilerParams(vmem_limit_bytes=16 << 20),
        name="turned",
    )(*[near_by(v) for v in values])


def gradient_kernel(steps, wanted, early, last, parts, *refs):
    outs = refs[: len(wanted)]
    place, hops = lax.axis_index("hop"), lax.axis_size("hop")
    core = lax.axis_index("core")
    _, pairs, rows, half = outs[0].shape
    span = pairs * rows
    blocks = []
    for step in steps:
        here = pl.ds(pl.multiple_of(((place + step) % hops) * span, span), span)
        blocks.append(jnp.concatenate([early[here, :], last[here, :]], axis=1))
    features = jnp.concatenate(blocks, axis=0)
    if len(wanted) > 1:
        whole = refs[-1]
        whole[...] = jnp.dot(features, parts[...], preferred_element_type=jnp.float32)
    for name, target in zip(wanted, outs):
        side = core if name == "kept" else 1 - core
        columns = pl.ds(pl.multiple_of(side * half, 128), half)
        if len(wanted) == 1:
            total = jnp.dot(features, parts[:, columns], preferred_element_type=jnp.float32)
        for index in range(len(steps)):
            for pair in range(pairs):
                start = (index * pairs + pair) * rows
                lines = slice(start, start + rows)
                value = total[lines] if len(wanted) == 1 else whole[lines, columns]
                target[index, pair] = value.astype(target.dtype)


def partial_gradient(steps, wanted, frames, early, last, parts):
    vmem = pl.BlockSpec(memory_space=pltpu.VMEM)
    features, width = early.shape[0], parts.shape[1]
    rows = features // frames
    pairs = lax.axis_size("side")
    shape = (len(steps), pairs, rows, width // 2)
    kinds = {"kept": jnp.float32, "sent": jnp.bfloat16}
    scratch = [pltpu.VMEM((len(steps) * pairs * rows, width), jnp.float32)]
    return pl.pallas_call(
        functools.partial(gradient_kernel, steps, wanted),
        in_specs=[vmem] * 3,
        out_specs=[vmem] * len(wanted),
        out_shape=[pltpu.VMEM(shape, kinds[name]) for name in wanted],
        scratch_shapes=scratch if len(wanted) > 1 else [],
        compiler_params=pltpu.CompilerParams(vmem_limit_bytes=24 << 20),
        name="partial_gradient",
    )(*[near_by(a) for a in (early, last, parts)])


def body(
    inputs,
    query_states,
    key_states,
    value_states,
    out_grad,
    first_flags,
    weight,
    moment_one,
    moment_two,
):
    hops, pairs = lax.axis_size("hop"), lax.axis_size("side")
    frames = hops * pairs
    swap = [(0, 1), (1, 0)]

    own = (key_states[0], value_states[0], inputs[0])
    tokens = own[0].shape[0]
    cut = tokens * 9 // 20 // 16 * 16
    spans = ((0, cut), (cut, tokens - cut))
    first = cut_out(own[:1], (spans[:1],))
    pieces = [*first, *cut_out(own, (spans[1:], spans, spans))]

    def behind(value, index):
        far = lax.ppermute(value, ("hop", "side"), [(i, i + 2) for i in range(frames - 2)])
        mixed = picked(far, own[index // 2], spans[index % 2][0])
        near = lax.ppermute(mixed, "side", swap)
        return far, near

    moved = [behind(piece, index) for index, piece in enumerate(pieces)]
    keys, values, features = (
        (whole, *zip(*moved[2 * i : 2 * i + 2])) for i, whole in enumerate(own)
    )
    early = turned(features[0], *features[1])
    parts = key_grads(
        first_flags,
        query_states[0],
        out_grad[0],
        (keys[0], *keys[1], *keys[2]),
        (values[0], *values[1], *values[2]),
    )
    last = turned(*features[2])
    stays, comes = [], []
    for steps, name in zip(groups_of(hops), STREAM):
        product = functools.partial(partial_gradient, steps)
        window = (frames, early, last, parts)
        if name == STREAM[0]:
            (sent,), (kept,) = product(("sent",), *window), product(("kept",), *window)
        else:
            kept, sent = product(("kept", "sent"), *window)
        taken = lax.ppermute(sent, "core", swap)
        kept, sent = by_side(kept, taken)
        taken = lax.ppermute(sent, "side", swap)
        send_on(steps, kept, taken, stays, comes)
    mine = small_call(add_kernel, *stays, *comes, out=thin(stays[0].shape))
    own, other = over_clip(mine, swap)
    state = (weight, moment_one, moment_two)
    outs = update_columns("own", own, state)
    return update_columns("other", other, state, outs)


def groups_of(hops):
    if hops > 4:
        return (tuple(range(hops)),)
    order = (*sorted(range(1, hops), key=lambda k: -min(k, hops - k)), 0)
    return tuple(group for group in (order[: hops // 2], order[hops // 2 :]) if group)


def send_on(steps, kept, taken, stays, comes):
    hops = lax.axis_size("hop")
    _, rows, half = kept.shape
    if hops > 4:
        kernel = functools.partial(line_kernel, steps)
        line = small_call(kernel, kept, taken, out=thin(kept.shape))
        stays.extend(lax.all_to_all(line, "hop", 0, 0))
        return
    outs = tuple(thin((rows, half)) if step else wide((rows, half)) for step in steps)
    blocks = small_call(by_hop_kernel, kept, taken, out=outs)
    for step, block in zip(steps, blocks):
        if step:
            route = [(i, (i + step) % hops) for i in range(hops)]
            comes.append(lax.ppermute(block, "hop", route))
        else:
            stays.append(block)


def small_call(kernel, *arrays, out):
    vmem = pl.BlockSpec(memory_space=pltpu.VMEM)
    return pl.pallas_call(
        kernel,
        in_specs=[vmem] * len(arrays),
        out_specs=jax.tree.map(lambda _: vmem, out),
        out_shape=out,
        compiler_params=pltpu.CompilerParams(vmem_limit_bytes=16 << 20),
    )(*arrays)


def wide(shape):
    return jax.ShapeDtypeStruct(shape, jnp.float32)


def thin(shape):
    return jax.ShapeDtypeStruct(shape, jnp.bfloat16)


def by_side_kernel(kept, taken, stay, leave):
    side = lax.axis_index("side")
    leave[...] = (kept[:, 1 - side] + taken[:, 1 - side].astype(jnp.float32)).astype(leave.dtype)
    stay[...] = kept[:, side] + taken[:, side].astype(jnp.float32)


def by_side(kept, taken):
    count, _, rows, half = kept.shape
    shape = (count, rows, half)
    return small_call(by_side_kernel, kept, taken, out=(wide(shape), thin(shape)))


def by_hop_kernel(kept, taken, *outs):
    for index, out in enumerate(outs):
        out[...] = (kept[index] + taken[index].astype(jnp.float32)).astype(out.dtype)


def line_kernel(steps, kept, taken, out):
    place, hops = lax.axis_index("hop"), lax.axis_size("hop")
    for index, step in enumerate(steps):
        total = kept[index] + taken[index].astype(jnp.float32)
        out[(place + step) % hops] = total.astype(out.dtype)


def add_kernel(first, *refs):
    *others, out = refs
    total = first[...].astype(jnp.float32)
    for other in others:
        total = total + other[...].astype(jnp.float32)
    out[...] = total.astype(out.dtype)


def over_clip(mine, swap):
    sets = lax.axis_size("set")
    if sets == 2:
        terms = (mine, lax.ppermute(mine, "set", swap))
    else:
        terms = tuple(lax.all_gather(mine, "set", axis=0, tiled=False))
    total = small_call(add_kernel, *terms, out=wide(mine.shape))
    return total, lax.ppermute(total, "core", swap)


def update_kernel(shift, part, *refs):
    state, outs, news, sems = refs[:3], refs[-9:-6], refs[-6:-3], refs[-3:]
    half = part.shape[1]
    side = (lax.axis_index("core") + shift) % 2
    columns = pl.ds(pl.multiple_of(side * half, 128), half)
    copies = []
    for out, new, sem, value in zip(
        outs, news, sems, adamw(*(ref[:, columns] for ref in state), part[...])
    ):
        new[...] = value
        copies.append(pltpu.make_async_copy(new, out.at[:, columns], sem))
        copies[-1].start()
    for copy in copies:
        copy.wait()


def update_columns(whose, part, state, outs=()):
    vmem, anywhere = (pl.BlockSpec(memory_space=space) for space in (pltpu.VMEM, pl.ANY))
    return pl.pallas_call(
        functools.partial(update_kernel, int(whose == "other")),
        in_specs=[vmem] * (1 + len(state)) + [anywhere] * len(outs),
        out_specs=(anywhere,) * 3,
        out_shape=(wide(state[0].shape),) * 3,
        scratch_shapes=[pltpu.VMEM(part.shape, part.dtype)] * 3 + [pltpu.SemaphoreType.DMA] * 3,
        input_output_aliases={1 + len(state) + i: i for i in range(len(outs))},
        compiler_params=pltpu.CompilerParams(vmem_limit_bytes=16 << 20),
    )(part, *state, *outs)


STREAM = ("one", "two", "three", "four", "five", "six")


def solution(mesh):
    clip, frames = mesh.shape["clip"], mesh.shape["tm"]
    grid = Mesh(
        mesh.devices.reshape(clip // 2, 2, frames // 2, 2), ("set", "core", "hop", "side")
    )
    seq, tok = ("set", "core"), ("hop", "side")
    wide = P(seq, tok, None)
    rows = P(tok, None)
    in_specs = (wide,) * 5 + (P(seq, None),) + (rows,) * 3

    return jax.shard_map(body, mesh=grid, in_specs=in_specs, out_specs=(rows,) * 3, check_vma=False)
```

```python
import functools
import math

import jax
import jax.numpy as jnp
from jax import lax
from jax.experimental import pallas as pl
from jax.experimental.pallas import tpu as pltpu
from jax.sharding import Mesh, PartitionSpec as P


HEAD_DIM = 128


beta_one = 0.9
beta_two = 0.95
learn_rate = 0.001
adam_eps = 1e-08
decay_rate = 0.1
step_count = 10.0

TOKENS_BOTH = (((1,), (1,)), ((), ()))


def adamw(weight, moment_one, moment_two, gradient):
    new_one = beta_one * moment_one + (1.0 - beta_one) * gradient
    new_two = beta_two * moment_two + (1.0 - beta_two) * gradient * gradient
    corr_one = new_one / (1.0 - beta_one**step_count)
    corr_two = new_two / (1.0 - beta_two**step_count)
    new_weight = weight - learn_rate * (
        corr_one / (jnp.sqrt(corr_two) + adam_eps) + decay_rate * weight
    )
    return (new_weight, new_one, new_two)


def near_by(value):
    return pltpu.with_memory_space_constraint(value, pltpu.VMEM)


def far_off(value):
    return pltpu.with_memory_space_constraint(value, pltpu.HBM)


def cut_kernel(spans, *refs):
    wholes, outs, sem = refs[: len(spans)], refs[len(spans) : -1], refs[-1]
    copies, index = [], 0
    for whole, rows in zip(wholes, spans):
        for start, size in rows:
            copies.append(
                pltpu.make_async_copy(whole.at[pl.ds(start, size)], outs[index], sem.at[index])
            )
            index += 1
    for copy in copies:
        copy.start()
    for copy in copies:
        copy.wait()


def cut_out(wholes, spans):
    anywhere = pl.BlockSpec(memory_space=pl.ANY)
    shapes = [
        jax.ShapeDtypeStruct((size, whole.shape[1]), whole.dtype)
        for whole, rows in zip(wholes, spans)
        for _, size in rows
    ]
    return pl.pallas_call(
        functools.partial(cut_kernel, spans),
        in_specs=[anywhere] * len(wholes),
        out_specs=[pl.BlockSpec(memory_space=pltpu.VMEM)] * len(shapes),
        out_shape=shapes,
        scratch_shapes=[pltpu.SemaphoreType.DMA((len(shapes),))],
        compiler_params=pltpu.CompilerParams(vmem_limit_bytes=4 << 20),
        name="cut_out",
    )(*[far_off(whole) for whole in wholes])


def pick_kernel(far, piece, out):
    side = lax.axis_index("side")

    @pl.when(side == 1)
    def _():
        out[...] = far[...]

    @pl.when(side != 1)
    def _():
        out[...] = piece[...]


def picked(far, piece):
    vmem = pl.BlockSpec(memory_space=pltpu.VMEM)
    return pl.pallas_call(
        pick_kernel,
        in_specs=[vmem, vmem],
        out_specs=vmem,
        out_shape=pltpu.VMEM(far.shape, far.dtype),
        compiler_params=pltpu.CompilerParams(vmem_limit_bytes=1 << 20),
        name="picked",
    )(near_by(far), near_by(piece))


def frame_index():
    return lax.axis_index("hop") * lax.axis_size("side") + lax.axis_index("side")


def folded(value):
    return value.reshape(value.shape[0] // 8, 8, value.shape[1])


def head_columns(refs, head):
    columns = slice(head * HEAD_DIM, (head + 1) * HEAD_DIM)
    parts = [ref[:, columns] for ref in refs]
    return parts[0] if len(parts) == 1 else jnp.concatenate(parts, axis=0)


def key_grads_kernel(key_cuts, val_cuts, flags, query, grad, *refs):
    keys, refs = refs[:key_cuts], refs[key_cuts:]
    values, refs = refs[:val_cuts], refs[val_cuts:]
    out, *scratch = refs
    scores, dprobs, raiseds, dscores = (scratch[i : i + 2] for i in (0, 2, 4, 6))
    rows, width = query.shape
    heads = width // HEAD_DIM
    lanes = scores[0].shape[1]
    scaling = 1.0 / math.sqrt(HEAD_DIM)
    power = scaling * math.log2(math.e)
    position = frame_index()
    near_ok = jnp.logical_and(position >= 1, flags[0, position] == 0)
    far_ok = jnp.logical_and(
        jnp.logical_and(near_ok, position >= 2), flags[0, jnp.maximum(position - 1, 0)] == 0
    )
    seen = (None, far_ok, near_ok)
    blank = jnp.zeros((lanes - rows, HEAD_DIM), query.dtype)
    step = 32 if rows % 32 == 0 else rows
    base = pl.multiple_of(jnp.minimum(flags[0, 0], 0) * 32, 32)

    def piece_of(start, size=step):
        return pl.ds(base + start, size)

    def padded(ref, head):
        return jnp.concatenate([head_columns([ref], head), blank], axis=0)

    def products(head):
        slot = head % 2
        for refs_of, other, target in ((keys, query, scores), (values, grad, dprobs)):
            target[slot][piece_of(0, 3 * rows), :] = lax.dot_general(
                head_columns(refs_of, head),
                padded(other, head),
                TOKENS_BOTH,
                preferred_element_type=jnp.float32,
            )

    def softmax(head):
        slot = head % 2
        tops = []
        for frame, ok in enumerate(seen):
            top = jnp.max(folded(scores[slot][piece_of(frame * rows, rows), :]), axis=0)
            tops.append(top if ok is None else jnp.where(ok, top, -jnp.inf))
        top = jnp.max(functools.reduce(jnp.maximum, tops), axis=0, keepdims=True) * power
        total = dots = 0.0
        for frame, ok in enumerate(seen):
            lift = top if ok is None else jnp.where(ok, top, jnp.inf)
            for start in range(frame * rows, (frame + 1) * rows, step):
                piece = piece_of(start)
                raised = jnp.exp2(scores[slot][piece, :] * power - lift)
                raiseds[slot][piece, :] = raised
                total = total + jnp.sum(folded(raised), axis=0)
                dots = dots + jnp.sum(folded(raised * dprobs[slot][piece, :]), axis=0)
        inverse = 1.0 / jnp.sum(total, axis=0, keepdims=True)
        delta = jnp.sum(dots, axis=0, keepdims=True) * inverse
        level = inverse * scaling
        for start in range(0, 3 * rows, step):
            piece = piece_of(start)
            value = raiseds[slot][piece, :] * level * (dprobs[slot][piece, :] - delta)
            dscores[slot][piece, :] = value.astype(dscores[slot].dtype)

    def collect(head):
        part = jnp.dot(
            dscores[head % 2][piece_of(0, 3 * rows), :],
            padded(query, head),
            preferred_element_type=jnp.float32,
        )
        out[:, head * HEAD_DIM : (head + 1) * HEAD_DIM] = part.astype(out.dtype)

    for beat in range(heads + 2):
        if beat >= 2:
            collect(beat - 2)
        if beat < heads:
            products(beat)
        if 1 <= beat <= heads:
            softmax(beat - 1)


def key_grads(flag_row, queries, grads, keys, values):
    rows, width = queries.shape
    lanes = pl.cdiv(rows, 128) * 128
    smem = pl.BlockSpec(memory_space=pltpu.SMEM)
    vmem = pl.BlockSpec(memory_space=pltpu.VMEM)
    arrays = [near_by(a) for a in (queries, grads, *keys, *values)]
    return pl.pallas_call(
        functools.partial(key_grads_kernel, len(keys), len(values)),
        in_specs=[smem] + [vmem] * len(arrays),
        out_specs=vmem,
        out_shape=pltpu.VMEM((3 * rows, width), jnp.bfloat16),
        scratch_shapes=[
            pltpu.VMEM((3 * rows, lanes), dtype)
            for dtype in (jnp.float32, jnp.float32, jnp.float32, jnp.bfloat16)
            for _ in range(2)
        ],
        compiler_params=pltpu.CompilerParams(vmem_limit_bytes=24 << 20),
        name="key_grads",
    )(flag_row, *arrays)


def turn_kernel(*refs):
    *values, out = refs
    out[...] = jnp.concatenate([v[...] for v in values], axis=0).T


def turned(*values):
    vmem = pl.BlockSpec(memory_space=pltpu.VMEM)
    tokens = sum(v.shape[0] for v in values)
    return pl.pallas_call(
        turn_kernel,
        in_specs=[vmem] * len(values),
        out_specs=vmem,
        out_shape=pltpu.VMEM((values[0].shape[1], tokens), values[0].dtype),
        compiler_params=pltpu.CompilerParams(vmem_limit_bytes=16 << 20),
        name="turned",
    )(*[near_by(v) for v in values])


def gradient_kernel(steps, wanted, early, last, parts, *refs):
    outs = refs[: len(wanted)]
    place, hops = lax.axis_index("hop"), lax.axis_size("hop")
    core = lax.axis_index("core")
    _, pairs, rows, half = outs[0].shape
    span = pairs * rows
    blocks = []
    for step in steps:
        here = pl.ds(pl.multiple_of(((place + step) % hops) * span, span), span)
        blocks.append(jnp.concatenate([early[here, :], last[here, :]], axis=1))
    features = jnp.concatenate(blocks, axis=0)
    if len(wanted) > 1:
        whole = refs[-1]
        whole[...] = jnp.dot(features, parts[...], preferred_element_type=jnp.float32)
    for name, target in zip(wanted, outs):
        side = core if name == "kept" else 1 - core
        columns = pl.ds(pl.multiple_of(side * half, 128), half)
        if len(wanted) == 1:
            total = jnp.dot(features, parts[:, columns], preferred_element_type=jnp.float32)
        for index in range(len(steps)):
            for pair in range(pairs):
                start = (index * pairs + pair) * rows
                lines = slice(start, start + rows)
                value = total[lines] if len(wanted) == 1 else whole[lines, columns]
                target[index, pair] = value.astype(target.dtype)


def partial_gradient(steps, wanted, frames, early, last, parts):
    vmem = pl.BlockSpec(memory_space=pltpu.VMEM)
    features, width = early.shape[0], parts.shape[1]
    rows = features // frames
    pairs = lax.axis_size("side")
    shape = (len(steps), pairs, rows, width // 2)
    kinds = {"kept": jnp.float32, "sent": jnp.bfloat16}
    scratch = [pltpu.VMEM((len(steps) * pairs * rows, width), jnp.float32)]
    return pl.pallas_call(
        functools.partial(gradient_kernel, steps, wanted),
        in_specs=[vmem] * 3,
        out_specs=[vmem] * len(wanted),
        out_shape=[pltpu.VMEM(shape, kinds[name]) for name in wanted],
        scratch_shapes=scratch if len(wanted) > 1 else [],
        compiler_params=pltpu.CompilerParams(vmem_limit_bytes=24 << 20),
        name="partial_gradient",
    )(*[near_by(a) for a in (early, last, parts)])


def body(
    inputs,
    query_states,
    key_states,
    value_states,
    out_grad,
    first_flags,
    weight,
    moment_one,
    moment_two,
):
    hops, pairs = lax.axis_size("hop"), lax.axis_size("side")
    frames = hops * pairs
    swap = [(0, 1), (1, 0)]

    own = (key_states[0], value_states[0], inputs[0])
    tokens = own[0].shape[0]
    cut = tokens * 9 // 20 // 16 * 16
    spans = ((0, cut), (cut, tokens - cut))
    first = cut_out(own[:1], (spans[:1],))
    pieces = [*first, *cut_out(own, (spans[1:], spans, spans))]

    def behind(value):
        far = lax.ppermute(value, ("hop", "side"), [(i, i + 2) for i in range(frames - 2)])
        mixed = picked(far, value)
        near = lax.ppermute(mixed, "side", swap)
        return far, near

    moved = [behind(piece) for piece in pieces]
    keys, values, features = (
        (whole, *zip(*moved[2 * i : 2 * i + 2])) for i, whole in enumerate(own)
    )
    early = turned(features[0], *features[1])
    parts = key_grads(
        first_flags,
        query_states[0],
        out_grad[0],
        (keys[0], *keys[1], *keys[2]),
        (values[0], *values[1], *values[2]),
    )
    last = turned(*features[2])
    stays, comes = [], []
    for steps, name in zip(groups_of(hops), STREAM):
        product = functools.partial(partial_gradient, steps)
        window = (frames, early, last, parts)
        if name == STREAM[0]:
            (sent,), (kept,) = product(("sent",), *window), product(("kept",), *window)
        else:
            kept, sent = product(("kept", "sent"), *window)
        taken = lax.ppermute(sent, "core", swap)
        kept, sent = by_side(kept, taken)
        taken = lax.ppermute(sent, "side", swap)
        send_on(steps, kept, taken, stays, comes)
    mine = small_call(add_kernel, *stays, *comes, out=thin(stays[0].shape))
    own, other = over_clip(mine, swap)
    state = (weight, moment_one, moment_two)
    outs = update_columns("own", own, state)
    return update_columns("other", other, state, outs)


def groups_of(hops):
    if hops > 4:
        return (tuple(range(hops)),)
    order = (*sorted(range(1, hops), key=lambda k: -min(k, hops - k)), 0)
    return tuple(group for group in (order[: hops // 2], order[hops // 2 :]) if group)


def send_on(steps, kept, taken, stays, comes):
    hops = lax.axis_size("hop")
    _, rows, half = kept.shape
    if hops > 4:
        kernel = functools.partial(line_kernel, steps)
        line = small_call(kernel, kept, taken, out=thin(kept.shape))
        stays.extend(lax.all_to_all(line, "hop", 0, 0))
        return
    outs = tuple(thin((rows, half)) if step else wide((rows, half)) for step in steps)
    blocks = small_call(by_hop_kernel, kept, taken, out=outs)
    for step, block in zip(steps, blocks):
        if step:
            route = [(i, (i + step) % hops) for i in range(hops)]
            comes.append(lax.ppermute(block, "hop", route))
        else:
            stays.append(block)


def small_call(kernel, *arrays, out):
    vmem = pl.BlockSpec(memory_space=pltpu.VMEM)
    return pl.pallas_call(
        kernel,
        in_specs=[vmem] * len(arrays),
        out_specs=jax.tree.map(lambda _: vmem, out),
        out_shape=out,
        compiler_params=pltpu.CompilerParams(vmem_limit_bytes=16 << 20),
    )(*arrays)


def wide(shape):
    return jax.ShapeDtypeStruct(shape, jnp.float32)


def thin(shape):
    return jax.ShapeDtypeStruct(shape, jnp.bfloat16)


def by_side_kernel(kept, taken, stay, leave):
    side = lax.axis_index("side")
    leave[...] = (kept[:, 1 - side] + taken[:, 1 - side].astype(jnp.float32)).astype(leave.dtype)
    stay[...] = kept[:, side] + taken[:, side].astype(jnp.float32)


def by_side(kept, taken):
    count, _, rows, half = kept.shape
    shape = (count, rows, half)
    return small_call(by_side_kernel, kept, taken, out=(wide(shape), thin(shape)))


def by_hop_kernel(kept, taken, *outs):
    for index, out in enumerate(outs):
        out[...] = (kept[index] + taken[index].astype(jnp.float32)).astype(out.dtype)


def line_kernel(steps, kept, taken, out):
    place, hops = lax.axis_index("hop"), lax.axis_size("hop")
    for index, step in enumerate(steps):
        total = kept[index] + taken[index].astype(jnp.float32)
        out[(place + step) % hops] = total.astype(out.dtype)


def add_kernel(first, *refs):
    *others, out = refs
    total = first[...].astype(jnp.float32)
    for other in others:
        total = total + other[...].astype(jnp.float32)
    out[...] = total.astype(out.dtype)


def over_clip(mine, swap):
    sets = lax.axis_size("set")
    if sets == 2:
        terms = (mine, lax.ppermute(mine, "set", swap))
    else:
        terms = tuple(lax.all_gather(mine, "set", axis=0, tiled=False))
    total = small_call(add_kernel, *terms, out=wide(mine.shape))
    return total, lax.ppermute(total, "core", swap)


def update_kernel(shift, part, *refs):
    state, outs, news, sems = refs[:3], refs[-9:-6], refs[-6:-3], refs[-3:]
    half = part.shape[1]
    side = (lax.axis_index("core") + shift) % 2
    columns = pl.ds(pl.multiple_of(side * half, 128), half)
    copies = []
    for out, new, sem, value in zip(
        outs, news, sems, adamw(*(ref[:, columns] for ref in state), part[...])
    ):
        new[...] = value
        copies.append(pltpu.make_async_copy(new, out.at[:, columns], sem))
        copies[-1].start()
    for copy in copies:
        copy.wait()


def update_columns(whose, part, state, outs=()):
    vmem, anywhere = (pl.BlockSpec(memory_space=space) for space in (pltpu.VMEM, pl.ANY))
    return pl.pallas_call(
        functools.partial(update_kernel, int(whose == "other")),
        in_specs=[vmem] * (1 + len(state)) + [anywhere] * len(outs),
        out_specs=(anywhere,) * 3,
        out_shape=(wide(state[0].shape),) * 3,
        scratch_shapes=[pltpu.VMEM(part.shape, part.dtype)] * 3 + [pltpu.SemaphoreType.DMA] * 3,
        input_output_aliases={1 + len(state) + i: i for i in range(len(outs))},
        compiler_params=pltpu.CompilerParams(vmem_limit_bytes=16 << 20),
    )(part, *state, *outs)


STREAM = ("one", "two", "three", "four", "five", "six")


def solution(mesh):
    clip, frames = mesh.shape["clip"], mesh.shape["tm"]
    grid = Mesh(
        mesh.devices.reshape(clip // 2, 2, frames // 2, 2), ("set", "core", "hop", "side")
    )
    seq, tok = ("set", "core"), ("hop", "side")
    wide = P(seq, tok, None)
    rows = P(tok, None)
    in_specs = (wide,) * 5 + (P(seq, None),) + (rows,) * 3

    return jax.shard_map(body, mesh=grid, in_specs=in_specs, out_specs=(rows,) * 3, check_vma=False)
```

```python
import functools
import math

import jax
import jax.numpy as jnp
from jax import lax
from jax.experimental import pallas as pl
from jax.experimental.pallas import tpu as pltpu
from jax.sharding import Mesh, PartitionSpec as P


HEAD_DIM = 128


beta_one = 0.9
beta_two = 0.95
learn_rate = 0.001
adam_eps = 1e-08
decay_rate = 0.1
step_count = 10.0

TOKENS_BOTH = (((1,), (1,)), ((), ()))


def adamw(weight, moment_one, moment_two, gradient):
    new_one = beta_one * moment_one + (1.0 - beta_one) * gradient
    new_two = beta_two * moment_two + (1.0 - beta_two) * gradient * gradient
    corr_one = new_one / (1.0 - beta_one**step_count)
    corr_two = new_two / (1.0 - beta_two**step_count)
    new_weight = weight - learn_rate * (
        corr_one / (jnp.sqrt(corr_two) + adam_eps) + decay_rate * weight
    )
    return (new_weight, new_one, new_two)


def near_by(value):
    return pltpu.with_memory_space_constraint(value, pltpu.VMEM)


def far_off(value):
    return pltpu.with_memory_space_constraint(value, pltpu.HBM)


def cut_kernel(spans, *refs):
    wholes, outs, sem = refs[: len(spans)], refs[len(spans) : -1], refs[-1]
    copies, index = [], 0
    for whole, rows in zip(wholes, spans):
        for start, size in rows:
            copies.append(
                pltpu.make_async_copy(whole.at[pl.ds(start, size)], outs[index], sem.at[index])
            )
            index += 1
    for copy in copies:
        copy.start()
    for copy in copies:
        copy.wait()


def cut_out(wholes, spans):
    anywhere = pl.BlockSpec(memory_space=pl.ANY)
    shapes = [
        jax.ShapeDtypeStruct((size, whole.shape[1]), whole.dtype)
        for whole, rows in zip(wholes, spans)
        for _, size in rows
    ]
    return pl.pallas_call(
        functools.partial(cut_kernel, spans),
        in_specs=[anywhere] * len(wholes),
        out_specs=[pl.BlockSpec(memory_space=pltpu.VMEM)] * len(shapes),
        out_shape=shapes,
        scratch_shapes=[pltpu.SemaphoreType.DMA((len(shapes),))],
        compiler_params=pltpu.CompilerParams(vmem_limit_bytes=4 << 20),
        name="cut_out",
    )(*[far_off(whole) for whole in wholes])


def pick_kernel(far, piece, out):
    side = lax.axis_index("side")

    @pl.when(side == 1)
    def _():
        out[...] = far[...]

    @pl.when(side != 1)
    def _():
        out[...] = piece[...]


def picked(far, piece):
    vmem = pl.BlockSpec(memory_space=pltpu.VMEM)
    return pl.pallas_call(
        pick_kernel,
        in_specs=[vmem, vmem],
        out_specs=vmem,
        out_shape=pltpu.VMEM(far.shape, far.dtype),
        compiler_params=pltpu.CompilerParams(vmem_limit_bytes=1 << 20),
        name="picked",
    )(near_by(far), near_by(piece))


def frame_index():
    return lax.axis_index("hop") * lax.axis_size("side") + lax.axis_index("side")


def folded(value):
    return value.reshape(value.shape[0] // 8, 8, value.shape[1])


def head_columns(refs, head):
    columns = slice(head * HEAD_DIM, (head + 1) * HEAD_DIM)
    parts = [ref[:, columns] for ref in refs]
    return parts[0] if len(parts) == 1 else jnp.concatenate(parts, axis=0)


def key_grads_kernel(key_cuts, val_cuts, flags, query, grad, *refs):
    keys, refs = refs[:key_cuts], refs[key_cuts:]
    values, refs = refs[:val_cuts], refs[val_cuts:]
    out, *scratch = refs
    scores, dprobs, raiseds, dscores = (scratch[i : i + 2] for i in (0, 2, 4, 6))
    rows, width = query.shape
    heads = width // HEAD_DIM
    lanes = scores[0].shape[1]
    scaling = 1.0 / math.sqrt(HEAD_DIM)
    power = scaling * math.log2(math.e)
    position = frame_index()
    near_ok = jnp.logical_and(position >= 1, flags[0, position] == 0)
    far_ok = jnp.logical_and(
        jnp.logical_and(near_ok, position >= 2), flags[0, jnp.maximum(position - 1, 0)] == 0
    )
    seen = (None, far_ok, near_ok)
    blank = jnp.zeros((lanes - rows, HEAD_DIM), query.dtype)
    step = 32 if rows % 32 == 0 else rows
    base = pl.multiple_of(jnp.minimum(flags[0, 0], 0) * 32, 32)

    def piece_of(start, size=step):
        return pl.ds(base + start, size)

    def padded(ref, head):
        return jnp.concatenate([head_columns([ref], head), blank], axis=0)

    def products(head):
        slot = head % 2
        for refs_of, other, target in ((keys, query, scores), (values, grad, dprobs)):
            target[slot][piece_of(0, 3 * rows), :] = lax.dot_general(
                head_columns(refs_of, head),
                padded(other, head),
                TOKENS_BOTH,
                preferred_element_type=jnp.float32,
            )

    def softmax(head):
        slot = head % 2
        tops = []
        for frame, ok in enumerate(seen):
            top = jnp.max(folded(scores[slot][piece_of(frame * rows, rows), :]), axis=0)
            tops.append(top if ok is None else jnp.where(ok, top, -jnp.inf))
        top = jnp.max(functools.reduce(jnp.maximum, tops), axis=0, keepdims=True) * power
        total = dots = 0.0
        for frame, ok in enumerate(seen):
            lift = top if ok is None else jnp.where(ok, top, jnp.inf)
            for start in range(frame * rows, (frame + 1) * rows, step):
                piece = piece_of(start)
                raised = jnp.exp2(scores[slot][piece, :] * power - lift)
                raiseds[slot][piece, :] = raised
                total = total + jnp.sum(folded(raised), axis=0)
                dots = dots + jnp.sum(folded(raised * dprobs[slot][piece, :]), axis=0)
        inverse = 1.0 / jnp.sum(total, axis=0, keepdims=True)
        delta = jnp.sum(dots, axis=0, keepdims=True) * inverse
        level = inverse * scaling
        for start in range(0, 3 * rows, step):
            piece = piece_of(start)
            value = raiseds[slot][piece, :] * level * (dprobs[slot][piece, :] - delta)
            dscores[slot][piece, :] = value.astype(dscores[slot].dtype)

    def collect(head):
        part = jnp.dot(
            dscores[head % 2][piece_of(0, 3 * rows), :],
            padded(query, head),
            preferred_element_type=jnp.float32,
        )
        out[:, head * HEAD_DIM : (head + 1) * HEAD_DIM] = part.astype(out.dtype)

    for beat in range(heads + 2):
        if beat >= 2:
            collect(beat - 2)
        if beat < heads:
            products(beat)
        if 1 <= beat <= heads:
            softmax(beat - 1)


def key_grads(flag_row, queries, grads, keys, values):
    rows, width = queries.shape
    lanes = pl.cdiv(rows, 128) * 128
    smem = pl.BlockSpec(memory_space=pltpu.SMEM)
    vmem = pl.BlockSpec(memory_space=pltpu.VMEM)
    arrays = [near_by(a) for a in (queries, grads, *keys, *values)]
    return pl.pallas_call(
        functools.partial(key_grads_kernel, len(keys), len(values)),
        in_specs=[smem] + [vmem] * len(arrays),
        out_specs=vmem,
        out_shape=pltpu.VMEM((3 * rows, width), jnp.bfloat16),
        scratch_shapes=[
            pltpu.VMEM((3 * rows, lanes), dtype)
            for dtype in (jnp.float32, jnp.float32, jnp.float32, jnp.bfloat16)
            for _ in range(2)
        ],
        compiler_params=pltpu.CompilerParams(vmem_limit_bytes=24 << 20),
        name="key_grads",
    )(flag_row, *arrays)


def turn_kernel(*refs):
    *values, out = refs
    out[...] = jnp.concatenate([v[...] for v in values], axis=0).T


def turned(*values):
    vmem = pl.BlockSpec(memory_space=pltpu.VMEM)
    tokens = sum(v.shape[0] for v in values)
    return pl.pallas_call(
        turn_kernel,
        in_specs=[vmem] * len(values),
        out_specs=vmem,
        out_shape=pltpu.VMEM((values[0].shape[1], tokens), values[0].dtype),
        compiler_params=pltpu.CompilerParams(vmem_limit_bytes=16 << 20),
        name="turned",
    )(*[near_by(v) for v in values])


def gradient_kernel(steps, wanted, early, last, parts, *refs):
    outs = refs[: len(wanted)]
    place, hops = lax.axis_index("hop"), lax.axis_size("hop")
    core = lax.axis_index("core")
    _, pairs, rows, half = outs[0].shape
    span = pairs * rows
    blocks = []
    for step in steps:
        here = pl.ds(pl.multiple_of(((place + step) % hops) * span, span), span)
        blocks.append(jnp.concatenate([early[here, :], last[here, :]], axis=1))
    features = jnp.concatenate(blocks, axis=0)
    if len(wanted) > 1:
        whole = refs[-1]
        whole[...] = jnp.dot(features, parts[...], preferred_element_type=jnp.float32)
    for name, target in zip(wanted, outs):
        side = core if name == "kept" else 1 - core
        columns = pl.ds(pl.multiple_of(side * half, 128), half)
        if len(wanted) == 1:
            total = jnp.dot(features, parts[:, columns], preferred_element_type=jnp.float32)
        for index in range(len(steps)):
            for pair in range(pairs):
                start = (index * pairs + pair) * rows
                lines = slice(start, start + rows)
                value = total[lines] if len(wanted) == 1 else whole[lines, columns]
                target[index, pair] = value.astype(target.dtype)


def partial_gradient(steps, wanted, frames, early, last, parts):
    vmem = pl.BlockSpec(memory_space=pltpu.VMEM)
    features, width = early.shape[0], parts.shape[1]
    rows = features // frames
    pairs = lax.axis_size("side")
    shape = (len(steps), pairs, rows, width // 2)
    kinds = {"kept": jnp.float32, "sent": jnp.bfloat16}
    scratch = [pltpu.VMEM((len(steps) * pairs * rows, width), jnp.float32)]
    return pl.pallas_call(
        functools.partial(gradient_kernel, steps, wanted),
        in_specs=[vmem] * 3,
        out_specs=[vmem] * len(wanted),
        out_shape=[pltpu.VMEM(shape, kinds[name]) for name in wanted],
        scratch_shapes=scratch if len(wanted) > 1 else [],
        compiler_params=pltpu.CompilerParams(vmem_limit_bytes=24 << 20),
        name="partial_gradient",
    )(*[near_by(a) for a in (early, last, parts)])


def body(
    inputs,
    query_states,
    key_states,
    value_states,
    out_grad,
    first_flags,
    weight,
    moment_one,
    moment_two,
):
    hops, pairs = lax.axis_size("hop"), lax.axis_size("side")
    frames = hops * pairs
    swap = [(0, 1), (1, 0)]

    own = (key_states[0], value_states[0], inputs[0])
    tokens = own[0].shape[0]
    cuts = [tokens * part // 20 // 16 * 16 for part in FIRST_PIECE]
    spans = [((0, cut), (cut, tokens - cut)) for cut in cuts]
    first = cut_out(own[:1], (spans[0][:1],))
    pieces = [*first, *cut_out(own, (spans[0][1:], spans[1], spans[2]))]

    def behind(value):
        far = lax.ppermute(value, ("hop", "side"), [(i, i + 2) for i in range(frames - 2)])
        mixed = picked(far, value)
        near = lax.ppermute(mixed, "side", swap)
        return far, near

    moved = [behind(piece) for piece in pieces]
    keys, values, features = (
        (whole, *zip(*moved[2 * i : 2 * i + 2])) for i, whole in enumerate(own)
    )
    early = turned(features[0], *features[1])
    parts = key_grads(
        first_flags,
        query_states[0],
        out_grad[0],
        (keys[0], *keys[1], *keys[2]),
        (values[0], *values[1], *values[2]),
    )
    last = turned(*features[2])
    stays, comes = [], []
    for steps, name in zip(groups_of(hops), STREAM):
        product = functools.partial(partial_gradient, steps)
        window = (frames, early, last, parts)
        if name == STREAM[0]:
            (sent,), (kept,) = product(("sent",), *window), product(("kept",), *window)
        else:
            kept, sent = product(("kept", "sent"), *window)
        taken = lax.ppermute(sent, "core", swap)
        kept, sent = by_side(kept, taken)
        taken = lax.ppermute(sent, "side", swap)
        send_on(steps, kept, taken, stays, comes)
    mine = small_call(add_kernel, *stays, *comes, out=thin(stays[0].shape))
    own, other = over_clip(mine, swap)
    state = (weight, moment_one, moment_two)
    outs = update_columns("own", own, state)
    return update_columns("other", other, state, outs)


def groups_of(hops):
    if hops > 4:
        return (tuple(range(hops)),)
    order = (*range(1, hops), 0)
    return tuple(group for group in (order[: hops // 2], order[hops // 2 :]) if group)


def send_on(steps, kept, taken, stays, comes):
    hops = lax.axis_size("hop")
    _, rows, half = kept.shape
    if hops > 4:
        kernel = functools.partial(line_kernel, steps)
        line = small_call(kernel, kept, taken, out=thin(kept.shape))
        stays.extend(lax.all_to_all(line, "hop", 0, 0))
        return
    outs = tuple(thin((rows, half)) if step else wide((rows, half)) for step in steps)
    blocks = small_call(by_hop_kernel, kept, taken, out=outs)
    for step, block in zip(steps, blocks):
        if step:
            route = [(i, (i + step) % hops) for i in range(hops)]
            comes.append(lax.ppermute(block, "hop", route))
        else:
            stays.append(block)


def small_call(kernel, *arrays, out):
    vmem = pl.BlockSpec(memory_space=pltpu.VMEM)
    return pl.pallas_call(
        kernel,
        in_specs=[vmem] * len(arrays),
        out_specs=jax.tree.map(lambda _: vmem, out),
        out_shape=out,
        compiler_params=pltpu.CompilerParams(vmem_limit_bytes=16 << 20),
    )(*arrays)


def wide(shape):
    return jax.ShapeDtypeStruct(shape, jnp.float32)


def thin(shape):
    return jax.ShapeDtypeStruct(shape, jnp.bfloat16)


def by_side_kernel(kept, taken, stay, leave):
    side = lax.axis_index("side")
    leave[...] = (kept[:, 1 - side] + taken[:, 1 - side].astype(jnp.float32)).astype(leave.dtype)
    stay[...] = kept[:, side] + taken[:, side].astype(jnp.float32)


def by_side(kept, taken):
    count, _, rows, half = kept.shape
    shape = (count, rows, half)
    return small_call(by_side_kernel, kept, taken, out=(wide(shape), thin(shape)))


def by_hop_kernel(kept, taken, *outs):
    for index, out in enumerate(outs):
        out[...] = (kept[index] + taken[index].astype(jnp.float32)).astype(out.dtype)


def line_kernel(steps, kept, taken, out):
    place, hops = lax.axis_index("hop"), lax.axis_size("hop")
    for index, step in enumerate(steps):
        total = kept[index] + taken[index].astype(jnp.float32)
        out[(place + step) % hops] = total.astype(out.dtype)


def add_kernel(first, *refs):
    *others, out = refs
    total = first[...].astype(jnp.float32)
    for other in others:
        total = total + other[...].astype(jnp.float32)
    out[...] = total.astype(out.dtype)


def over_clip(mine, swap):
    sets = lax.axis_size("set")
    if sets == 2:
        terms = (mine, lax.ppermute(mine, "set", swap))
    else:
        terms = tuple(lax.all_gather(mine, "set", axis=0, tiled=False))
    total = small_call(add_kernel, *terms, out=wide(mine.shape))
    return total, lax.ppermute(total, "core", swap)


def update_kernel(shift, part, *refs):
    state, outs, news, sems = refs[:3], refs[-9:-6], refs[-6:-3], refs[-3:]
    half = part.shape[1]
    side = (lax.axis_index("core") + shift) % 2
    columns = pl.ds(pl.multiple_of(side * half, 128), half)
    copies = []
    for out, new, sem, value in zip(
        outs, news, sems, adamw(*(ref[:, columns] for ref in state), part[...])
    ):
        new[...] = value
        copies.append(pltpu.make_async_copy(new, out.at[:, columns], sem))
        copies[-1].start()
    for copy in copies:
        copy.wait()


def update_columns(whose, part, state, outs=()):
    vmem, anywhere = (pl.BlockSpec(memory_space=space) for space in (pltpu.VMEM, pl.ANY))
    return pl.pallas_call(
        functools.partial(update_kernel, int(whose == "other")),
        in_specs=[vmem] * (1 + len(state)) + [anywhere] * len(outs),
        out_specs=(anywhere,) * 3,
        out_shape=(wide(state[0].shape),) * 3,
        scratch_shapes=[pltpu.VMEM(part.shape, part.dtype)] * 3 + [pltpu.SemaphoreType.DMA] * 3,
        input_output_aliases={1 + len(state) + i: i for i in range(len(outs))},
        compiler_params=pltpu.CompilerParams(vmem_limit_bytes=16 << 20),
    )(part, *state, *outs)


FIRST_PIECE = (9, 11, 8)
STREAM = ("one", "two", "three", "four", "five", "six")


def solution(mesh):
    clip, frames = mesh.shape["clip"], mesh.shape["tm"]
    grid = Mesh(
        mesh.devices.reshape(clip // 2, 2, frames // 2, 2), ("set", "core", "hop", "side")
    )
    seq, tok = ("set", "core"), ("hop", "side")
    wide = P(seq, tok, None)
    rows = P(tok, None)
    in_specs = (wide,) * 5 + (P(seq, None),) + (rows,) * 3

    return jax.shard_map(body, mesh=grid, in_specs=in_specs, out_specs=(rows,) * 3, check_vma=False)
```
